32 devices in a mesh: rep: 2 (over core), own: 16 (over z, y, x).
Axes of the slice: x: 2, y: 2, z: 4, core: 2. Of those that a mesh axis runs over, the one named last changes fastest.
Arguments:
- weights: float32 [512, 8, 4096], P('own'), may hold values from -6 to 6
- differences: float32 [2, 512, 8, 4096], P('rep', 'own'), may hold values from -6 to 6
- bases: float32 [6, 4096, 64], replicated, may hold values from -0.09375 to 0.09375
- momentum: float32 [16, 16, 4, 8, 64], P('own'), may hold values from -6 to 6
- owners: int32 [512, 1], replicated, may hold values from 0 to 15; in each aligned block of 32 rows (0 to 31, 32 to 63, ...) at most 4 rows name the same one
- matrix_ids: int32 [512], replicated, may hold values from 0 to 5, never falling along the last dimension, each value on 1 to 127 neighbouring positions
Outputs:
- new_weights: float32 [512, 8, 4096], P('own')
- new_momentum: float32 [16, 16, 4, 8, 64], P('own')
The draws below stay inside these ranges and needn't reach their ends.
Inputs may be any that keep to these rules, and one draw needn't show every extreme that they name: `owners`: the 32 slabs of one holder name each owner at most 4 times, a bound that some block reaches. `matrix_ids`: never falling; each matrix has 1 to 127 slabs, one exactly that many.
All inputs are finite; a program needn't handle non-finite values.
Results may differ from the reference program's by a relative error of at most 0.0001.
Values sent between devices are 32-bit elements; how exact they have to be, the bound alone decides.
No kernel may reach another device: no remote copies, remote signals or barrier semaphores. Data moves between devices by JAX's collectives and lax.ppermute only.
A program may use at most 192 MiB of HBM per device.

```python
import math
import jax
import jax.numpy as jnp
import numpy as np
from jax import lax

D = 4096
R = 64
BR = 8
BLK_DEV = 32
MATS = 6
NBLK = 512
PEER = 4
GROUPS = 2
N_REP = 2
N_OWN = 16


def block_scale(key, dims, shards, least, high):
    gain, own = 1.0, jax.random.fold_in(key, 6)
    for position, parts in shards:
        heights = jnp.exp(jax.random.uniform(jax.random.fold_in(own, position), (parts,), jnp.float32, least / len(shards), high / len(shards)))
        gain = gain * jnp.repeat(heights, dims[position] // parts).reshape([-1 if axis == position else 1 for axis in range(len(dims))])
    return gain


def length_profile(amount, total, limit, slope):
    loads = [(1 << 20) // math.isqrt(standing ** slope) + 1 for standing in range(2, amount + 1)]
    spare, holding = total - limit - (amount - 1), [1] * (amount - 1)
    while spare > 0:
        movable = [i for i in range(amount - 1) if holding[i] < limit]
        pool, remaining = sum([loads[i] for i in movable]), spare
        for i in movable:
            extra = min(limit - holding[i], max(1, remaining * loads[i] // pool), spare)
            holding[i] = holding[i] + extra
            spare = spare - extra
    return np.array([limit] + holding)


def ragged_sizes(rng, count, total, most, lean):
    if count == 2:
        one = jax.random.randint(rng, (), max(1, total - most), min(most, total - 1) + 1)
        return jnp.stack([one, total - one])
    lengths = jnp.asarray(length_profile(count, total, most, lean), jnp.int32)
    pairs = (count - 1) // 2
    donor, sink = lengths[1:1 + 2 * pairs:2], lengths[2:2 + 2 * pairs:2]
    room = jnp.minimum(donor - 1, most - sink)
    shifted = jax.random.randint(jax.random.fold_in(rng, 1), (pairs,), 0, 1 << 20) % (room + 1)
    lengths = lengths.at[1:1 + 2 * pairs:2].set(donor - shifted).at[2:2 + 2 * pairs:2].set(sink + shifted)
    return lengths[jax.random.permutation(jax.random.fold_in(rng, 2), count)]


def deal_out(key, own, number, rows, amount, top, bound, slope):
    ranking = jax.random.permutation(key, amount)
    packed, common = load_shares(amount, rows * top, bound, slope, True), load_shares(amount, rows * top, bound, slope, False)
    places = jnp.arange(amount)

    def named(sizes, turn):
        used = int((sizes > 0).sum())
        fixed = max(1, used // 4)
        passed = fixed + (places - fixed + turn * (used - fixed)) % max(1, amount - fixed)
        return jnp.zeros((amount,), jnp.int32).at[ranking[jnp.where(places < fixed, places, passed)]].set(jnp.asarray(sizes, jnp.int32))

    sizes = jnp.where(number % 4 == 0, named(packed, number // 4), named(common, number - number // 4 - 1))
    mixed = jax.random.permutation(jax.random.fold_in(own, 3), amount)
    donor, taker = mixed[0:amount // 2 * 2:2], mixed[1:amount // 2 * 2:2]
    room = jnp.minimum(sizes[donor] - 1, bound - sizes[taker]) // 2
    room = jnp.where((donor == ranking[0]) | (taker == ranking[0]) | (sizes[taker] == 0), 0, jnp.maximum(room, 0))
    passed = jax.random.randint(jax.random.fold_in(own, 4), (amount // 2,), 0, 1 << 20) % (room + 1)
    sizes = sizes.at[donor].add(-passed).at[taker].add(passed)
    members = jnp.searchsorted(jnp.cumsum(sizes), jnp.arange(rows * top), side="right").astype(jnp.int32)
    listing = members.reshape(top, rows).T
    listing = listing[jax.random.permutation(jax.random.fold_in(own, 1), rows)]
    turn = jax.random.randint(jax.random.fold_in(own, 2), (rows, 1), 0, top)
    return jnp.take_along_axis(listing, (jnp.arange(top)[None, :] + turn) % top, axis=1)


def load_shares(count, total, most, lean, full):
    weights = [(1 << 20) // math.isqrt(rank ** lean) + 1 for rank in range(1, count + 1)]
    largest = most if full else min(most, max(-(-total // count), total * weights[0] // sum(weights)))
    least = 1 if total - largest >= count - 1 else 0
    holding, surplus = [largest] + [least] * (count - 1), total - largest - least * (count - 1)
    while surplus > 0:
        movable = [i for i in range(1, count) if holding[i] < largest] or [i for i in range(1, count) if holding[i] < most]
        whole, budget = sum([weights[i] for i in movable]), surplus
        for i in movable:
            more = min(most - holding[i], max(1, budget * weights[i] // whole), surplus)
            holding[i] = holding[i] + more
            surplus = surplus - more
    return np.array(holding)


def centred(key, extent, spread, most, pieces=(), kind=jnp.bfloat16):
    drawn = spread * jax.random.normal(key, extent, jnp.float32)
    if pieces:
        drawn = drawn * block_scale(key, extent, pieces, -0.22, 0.18)
    return jnp.clip(drawn, -most, most).astype(kind)


def setup_inputs(seed: int = 0) -> dict:
    keys = jax.random.split(jax.random.key(seed), 7)
    weights = centred(keys[0], (NBLK, BR, D), 1.0, 6.0, ((0, 16),), jnp.float32)
    differences = centred(keys[1], (GROUPS, NBLK, BR, D), 1.0, 6.0, ((0, 2), (1, 16)), jnp.float32)
    bases = centred(keys[2], (MATS, D, R), D ** -0.5, 0.09375, (), jnp.float32)
    momentum = centred(keys[3], (N_OWN, N_OWN, PEER, BR, R), 1.0, 6.0, ((0, 16),), jnp.float32)
    owners_keys = jax.random.split(jax.random.fold_in(keys[4], 1), NBLK // BLK_DEV)
    owners_turns = jax.random.permutation(jax.random.fold_in(keys[4], 3), NBLK // BLK_DEV)
    owners = jax.vmap(lambda own, number: deal_out(jax.random.fold_in(keys[4], 2), own, number, BLK_DEV, N_OWN, 1, PEER, 2))(owners_keys, owners_turns).reshape((NBLK, 1))
    matrix_ids = jnp.searchsorted(jnp.cumsum(ragged_sizes(keys[5], MATS, NBLK, NBLK // MATS + NBLK // (2 * MATS), 2)), jnp.arange(NBLK), side="right").astype(jnp.int32)
    return dict(weights=weights, differences=differences, bases=bases, momentum=momentum, owners=owners, matrix_ids=matrix_ids)


outer_rate = 0.7
decay_rate = 0.9


def reference(weights, differences, bases, momentum, owners, matrix_ids):
    owner_all = owners[:, 0].reshape(N_OWN, BLK_DEV)
    ownhot = (owner_all[:, :, None] == jnp.arange(N_OWN, dtype=jnp.int32)[None, None, :]).astype(jnp.int32)
    rank = jnp.sum(ownhot * (jnp.cumsum(ownhot, axis=1).astype(jnp.int32) - ownhot), axis=2)
    slot = owner_all * PEER + rank
    slothot = (slot[:, :, None] == jnp.arange(N_OWN * PEER, dtype=jnp.int32)[None, None, :]).astype(jnp.float32)
    mathot = (matrix_ids[:, None] == jnp.arange(MATS, dtype=jnp.int32)[None, :]).astype(jnp.float32)
    factors = jnp.zeros((NBLK, BR, R), jnp.float32)
    for index in range(MATS):
        proj = jnp.einsum('gnbd,dr->nbr', differences, bases[index], precision=lax.Precision.HIGHEST)
        factors = factors + mathot[:, index][:, None, None] * proj
    average = (factors / N_REP).reshape(N_OWN, BLK_DEV, BR, R)
    placed = jnp.einsum('hkc,hkbr->chbr', slothot, average, precision=lax.Precision.HIGHEST)
    placed = placed.reshape(N_OWN, PEER, N_OWN, BR, R).transpose(0, 2, 1, 3, 4)
    new_momentum = decay_rate * momentum + placed
    step = placed + decay_rate * new_momentum
    step_c = step.transpose(0, 2, 1, 3, 4).reshape(N_OWN * PEER, N_OWN, BR, R)
    picked = jnp.einsum('hkc,chbr->hkbr', slothot, step_c, precision=lax.Precision.HIGHEST).reshape(NBLK, BR, R)
    update = jnp.zeros((NBLK, BR, D), jnp.float32)
    for index in range(MATS):
        part = jnp.einsum('nbr,dr->nbd', picked, bases[index], precision=lax.Precision.HIGHEST)
        update = update + mathot[:, index][:, None, None] * part
    return weights - outer_rate * update, new_momentum
```

```python
import jax
import jax.numpy as jnp
from jax import lax
from jax.experimental import pallas as pl
from jax.experimental.pallas import tpu as pltpu
from jax.sharding import PartitionSpec as P

outer_rate = 0.7
decay_rate = 0.9
CHUNKS = 4
VMEM_LIMIT = 20 << 20
HOLD_LIMIT = 58 << 20


def split_parts(value):
    high = value.astype(jnp.bfloat16)
    low = (value - high.astype(jnp.float32)).astype(jnp.bfloat16)
    return high, low


def id_span(ids_ref, base, blocks):
    first = ids_ref[base]
    last = ids_ref[base + blocks - 1]
    return first, last


def slabs_upto(ids_ref, base, blocks, index):
    total = jnp.int32(0)
    for k in range(blocks):
        total = total + jnp.where(ids_ref[base + k] <= index, 1, 0)
    return total


def dot_nt(a, b):
    return lax.dot_general(a, b, (((1,), (1,)), ((), ())), preferred_element_type=jnp.float32)


def project_kernel(ids_ref, x_hbm, b_hbm, f_ref, xbuf, bbuf, xhi, xlo, acc, fac, xsem, bsem):
    blocks = x_hbm.shape[0] // 8
    rank = b_hbm.shape[1]
    width = xbuf.shape[2]
    base = lax.axis_index("own") * blocks
    first, last = id_span(ids_ref, base, blocks)
    pairs = (last - first + 2) // 2

    def x_copy(c):
        return pltpu.make_async_copy(
            x_hbm.at[:, pl.ds(c * width, width)], xbuf.at[c], xsem.at[c]
        )

    def b_copy(index, t, c):
        return pltpu.make_async_copy(
            b_hbm.at[index, :, pl.ds(c * width, width)], bbuf.at[t, c], bsem.at[t, c]
        )

    second = jnp.minimum(first + 1, last)
    for c in range(CHUNKS):
        b_copy(first, 0, c).start()
        b_copy(second, 1, c).start()
        x_copy(c).start()

    rows = lax.broadcasted_iota(jnp.int32, fac.shape, 0)

    def pair_step(p, carry):
        m0 = first + 2 * p
        m1 = jnp.minimum(m0 + 1, last)

        @pl.when(p > 0)
        def _():
            for c in range(CHUNKS):
                b_copy(m0, 0, c).start()
                b_copy(m1, 1, c).start()

        for c in range(CHUNKS):
            b_copy(m0, 0, c).wait()
            b_copy(m1, 1, c).wait()

            @pl.when(p == 0)
            def _():
                x_copy(c).wait()
                high, low = split_parts(xbuf[c])
                xhi[c] = high
                xlo[c] = low

            h0, l0 = split_parts(bbuf[0, c])
            h1, l1 = split_parts(bbuf[1, c])
            basis = jnp.concatenate([h0, l0, h1, l1], axis=0)
            part = dot_nt(xhi[c], basis) + dot_nt(xlo[c], basis)
            if c == 0:
                acc[...] = part
            else:
                acc[...] += part
        total = acc[...]
        f0 = total[:, 0:rank] + total[:, rank : 2 * rank]
        f1 = total[:, 2 * rank : 3 * rank] + total[:, 3 * rank : 4 * rank]
        low_edge = 8 * slabs_upto(ids_ref, base, blocks, m0 - 1)
        high_edge = 8 * slabs_upto(ids_ref, base, blocks, m0)
        kept = jnp.where(rows < high_edge, f0, f1)
        fac[...] = jnp.where(rows < low_edge, fac[...], kept)
        return carry

    lax.fori_loop(0, pairs, pair_step, 0)
    half = fac.shape[0] // 2
    f_ref[...] = jnp.concatenate([fac[0:half, :], fac[half : 2 * half, :]], axis=1)


def project_slabs(ids, diff, bases_t):
    rows, width = diff.shape
    rank = bases_t.shape[1]
    chunk = width // CHUNKS
    return pl.pallas_call(
        project_kernel,
        out_shape=jax.ShapeDtypeStruct((rows // 2, 2 * rank), jnp.float32),
        in_specs=[
            pl.BlockSpec(memory_space=pltpu.SMEM),
            pl.BlockSpec(memory_space=pltpu.HBM),
            pl.BlockSpec(memory_space=pltpu.HBM),
        ],
        out_specs=pl.BlockSpec(memory_space=pltpu.VMEM),
        scratch_shapes=[
            pltpu.VMEM((CHUNKS, rows, chunk), jnp.float32),
            pltpu.VMEM((2, CHUNKS, rank, chunk), jnp.float32),
            pltpu.VMEM((CHUNKS, rows, chunk), jnp.bfloat16),
            pltpu.VMEM((CHUNKS, rows, chunk), jnp.bfloat16),
            pltpu.VMEM((rows, 4 * rank), jnp.float32),
            pltpu.VMEM((rows, rank), jnp.float32),
            pltpu.SemaphoreType.DMA((CHUNKS,)),
            pltpu.SemaphoreType.DMA((2, CHUNKS)),
        ],
        compiler_params=pltpu.CompilerParams(vmem_limit_bytes=HOLD_LIMIT),
        cost_estimate=pl.CostEstimate(
            flops=6 * rows * width * rank, bytes_accessed=6 << 20, transcendentals=0
        ),
        name="project_slabs",
    )(ids, diff, bases_t)


def count_ranks(owners_ref, count_ref, base, blocks, visit):
    for n in range(count_ref.shape[0]):
        count_ref[n] = 0
    for k in range(blocks):
        owner = owners_ref[0, base + k]
        rank = count_ref[owner]
        count_ref[owner] = rank + 1
        visit(k, owner, rank)


def pack_kernel(owners_ref, mine_ref, other_ref, mom_ref, out_ref, avg_ref, count_ref):
    n_own, _, lanes = out_ref.shape
    rank = lanes // 2
    blocks = avg_ref.shape[0] // 8
    base = lax.axis_index("own") * blocks
    average = (mine_ref[...] + other_ref[...]) * 0.5
    half = average.shape[0]
    avg_ref[0:half, :] = average[:, 0:rank]
    avg_ref[half : 2 * half, :] = average[:, rank : 2 * rank]
    mom = mom_ref[...].reshape(out_ref.shape[0], out_ref.shape[1], rank)
    out_ref[...] = jnp.concatenate([jnp.zeros_like(mom), mom], axis=2)

    def visit(k, owner, slot):
        out_ref[owner, pl.ds(pl.multiple_of(slot * 8, 8), 8), 0:rank] = avg_ref[8 * k : 8 * k + 8, :]

    count_ranks(owners_ref, count_ref, base, blocks, visit)


def pack_factors(owners, mine, other, momentum):
    n_own, peer, br, rank = momentum.shape
    rows = 2 * mine.shape[0]
    vmem = pl.BlockSpec(memory_space=pltpu.VMEM)
    smem = pl.BlockSpec(memory_space=pltpu.SMEM)
    return pl.pallas_call(
        pack_kernel,
        out_shape=(
            jax.ShapeDtypeStruct((n_own, peer * br, 2 * rank), jnp.float32),
            jax.ShapeDtypeStruct((rows, rank), jnp.float32),
        ),
        in_specs=[smem, vmem, vmem, vmem],
        out_specs=(vmem, vmem),
        scratch_shapes=[pltpu.SMEM((n_own,), jnp.int32)],
        compiler_params=pltpu.CompilerParams(vmem_limit_bytes=4 << 20),
        name="pack_factors",
    )(owners, mine, other, momentum)


def rebuild_kernel(
    ids_ref, owners_ref, recv_ref, avg_ref, mom_ref, w_hbm, b_hbm, nm_ref, out_hbm,
    wbuf, bbuf, lhs, gath, count_ref, wsem, osem, bsem,
):
    rank = lhs.shape[2] // 2
    blocks = avg_ref.shape[0] // 8
    width = wbuf.shape[2]
    base = lax.axis_index("own") * blocks
    first, last = id_span(ids_ref, base, blocks)
    total = last - first + 1

    def w_copy(c):
        return pltpu.make_async_copy(
            w_hbm.at[:, pl.ds(c * width, width)], wbuf.at[c], wsem.at[c]
        )

    def o_copy(c):
        return pltpu.make_async_copy(
            wbuf.at[c], out_hbm.at[:, pl.ds(c * width, width)], osem.at[c]
        )

    def b_copy(t):
        return pltpu.make_async_copy(b_hbm.at[first + t], bbuf.at[t], bsem.at[t])

    for t in range(bbuf.shape[0]):

        @pl.when(t < total)
        def _():
            b_copy(t).start()

    for c in range(CHUNKS):
        w_copy(c).start()

    def visit(k, owner, slot):
        gath[8 * k : 8 * k + 8, :] = recv_ref[owner, pl.ds(pl.multiple_of(slot * 8, 8), 8), :]

    count_ranks(owners_ref, count_ref, base, blocks, visit)
    received = recv_ref[...]
    nm_ref[...] = decay_rate * mom_ref[...] + received[:, :, 0:rank].reshape(mom_ref.shape)
    placed = avg_ref[...]
    held = decay_rate * gath[:, rank : 2 * rank] + placed
    step = -outer_rate * (placed + decay_rate * held)
    rows = lax.broadcasted_iota(jnp.int32, step.shape, 0)
    for t in range(bbuf.shape[0]):

        @pl.when(t < total)
        def _():
            low_edge = 8 * slabs_upto(ids_ref, base, blocks, first + t - 1)
            high_edge = 8 * slabs_upto(ids_ref, base, blocks, first + t)
            chosen = jnp.where((rows >= low_edge) & (rows < high_edge), step, 0.0)
            high, low = split_parts(chosen)
            lhs[t] = jnp.concatenate([high, low], axis=1)
            b_copy(t).wait()

    for c in range(CHUNKS):
        w_copy(c).wait()

        def add_matrix(t, carry):
            high, low = split_parts(bbuf[t, :, pl.ds(c * width, width)])
            basis = jnp.concatenate([high, high, low, low], axis=0)
            left = lhs[t]
            wbuf[c] += jnp.dot(
                jnp.concatenate([left, left], axis=1), basis, preferred_element_type=jnp.float32
            )
            return carry

        lax.fori_loop(0, total, add_matrix, 0)
        o_copy(c).start()
    for c in range(CHUNKS):
        o_copy(c).wait()


def rebuild_slabs(ids, owners, received, average, momentum, weights, bases_t):
    rows, width = weights.shape
    mats, rank, _ = bases_t.shape
    n_own = momentum.shape[0]
    chunk = width // CHUNKS
    vmem = pl.BlockSpec(memory_space=pltpu.VMEM)
    smem = pl.BlockSpec(memory_space=pltpu.SMEM)
    hbm = pl.BlockSpec(memory_space=pltpu.HBM)
    return pl.pallas_call(
        rebuild_kernel,
        out_shape=(
            jax.ShapeDtypeStruct(momentum.shape, jnp.float32),
            jax.ShapeDtypeStruct(weights.shape, jnp.float32),
        ),
        in_specs=[smem, smem, vmem, vmem, vmem, hbm, hbm],
        out_specs=(vmem, hbm),
        scratch_shapes=[
            pltpu.VMEM((CHUNKS, rows, chunk), jnp.float32),
            pltpu.VMEM((mats, rank, width), jnp.float32),
            pltpu.VMEM((mats, rows, 2 * rank), jnp.bfloat16),
            pltpu.VMEM((rows, 2 * rank), jnp.float32),
            pltpu.SMEM((n_own,), jnp.int32),
            pltpu.SemaphoreType.DMA((CHUNKS,)),
            pltpu.SemaphoreType.DMA((CHUNKS,)),
            pltpu.SemaphoreType.DMA((mats,)),
        ],
        compiler_params=pltpu.CompilerParams(vmem_limit_bytes=VMEM_LIMIT),
        cost_estimate=pl.CostEstimate(
            flops=8 * rows * width * rank, bytes_accessed=10 << 20, transcendentals=0
        ),
        name="rebuild_slabs",
    )(ids, owners, received, average, momentum, weights, bases_t)


def per_device(weights, differences, bases, momentum, owners, matrix_ids):
    blocks, br, width = weights.shape
    n_rep = lax.axis_size("rep")
    bases_t = jnp.swapaxes(bases, 1, 2)
    owner_row = owners.T
    mine = project_slabs(matrix_ids, differences.reshape(blocks * br, width), bases_t)
    other = lax.ppermute(mine, "rep", [(i, n_rep - 1 - i) for i in range(n_rep)])
    packed, average = pack_factors(owner_row, mine, other, momentum[0])
    received = lax.all_to_all(packed, "own", split_axis=0, concat_axis=0, tiled=True)
    new_momentum, new_weights = rebuild_slabs(
        matrix_ids, owner_row, received, average, momentum[0],
        weights.reshape(blocks * br, width), bases_t,
    )
    return (new_weights.reshape(weights.shape), new_momentum[None])


def solution(mesh):
    placed = (
        P("own", None, None),
        P("rep", "own", None, None),
        P(),
        P("own", None, None, None, None),
        P(),
        P(),
    )
    return jax.shard_map(
        per_device,
        mesh=mesh,
        in_specs=placed,
        out_specs=(P("own", None, None), P("own", None, None, None, None)),
        check_vma=False,
    )
```

```python
import jax
import jax.numpy as jnp
from jax import lax
from jax.experimental import pallas as pl
from jax.experimental.pallas import tpu as pltpu
from jax.sharding import PartitionSpec as P

outer_rate = 0.7
decay_rate = 0.9
CHUNKS = 4
VMEM_LIMIT = 20 << 20


def split_parts(value):
    high = value.astype(jnp.bfloat16)
    low = (value - high.astype(jnp.float32)).astype(jnp.bfloat16)
    return high, low


def id_span(ids_ref, base, blocks):
    first = ids_ref[base]
    last = ids_ref[base + blocks - 1]
    return first, last


def slabs_upto(ids_ref, base, blocks, index):
    total = jnp.int32(0)
    for k in range(blocks):
        total = total + jnp.where(ids_ref[base + k] <= index, 1, 0)
    return total


def dot_nt(a, b):
    return lax.dot_general(a, b, (((1,), (1,)), ((), ())), preferred_element_type=jnp.float32)


def project_kernel(
    ids_hbm, x_hbm, b_hbm, f_ref, split_ref, ids_ref, xbuf, bbuf, fac, isem, xsem, bsem
):
    blocks = x_hbm.shape[0] // 8
    rank = b_hbm.shape[1]
    base = lax.axis_index("own") * blocks
    ids_copy = pltpu.make_async_copy(ids_hbm, ids_ref, isem)
    x_copy = pltpu.make_async_copy(x_hbm, xbuf, xsem)
    ids_copy.start()
    x_copy.start()

    def b_copy(index, t):
        return pltpu.make_async_copy(b_hbm.at[index], bbuf.at[t], bsem.at[t])

    ids_copy.wait()
    first, last = id_span(ids_ref, base, blocks)
    pairs = (last - first + 2) // 2
    b_copy(first, 0).start()
    b_copy(jnp.minimum(first + 1, last), 1).start()
    x_copy.wait()
    rows = lax.broadcasted_iota(jnp.int32, fac.shape, 0)

    def pair_step(p, carry):
        m0 = first + 2 * p
        m1 = jnp.minimum(m0 + 1, last)
        low_edge = 8 * slabs_upto(ids_ref, base, blocks, m0 - 1)
        high_edge = 8 * slabs_upto(ids_ref, base, blocks, m0)

        @pl.when(p > 0)
        def _():
            b_copy(m0, 0).start()
            b_copy(m1, 1).start()

        b_copy(m0, 0).wait()
        b_copy(m1, 1).wait()
        first_basis = jnp.concatenate(split_parts(bbuf[0]), axis=0)
        second_basis = jnp.concatenate(split_parts(bbuf[1]), axis=0)
        split_ref[2 * p] = first_basis
        split_ref[2 * p + 1] = second_basis
        basis = jnp.concatenate([first_basis, second_basis], axis=0)
        high, low = split_parts(xbuf[...])
        total = dot_nt(high, basis) + dot_nt(low, basis)
        f0 = total[:, 0:rank] + total[:, rank : 2 * rank]
        f1 = total[:, 2 * rank : 3 * rank] + total[:, 3 * rank : 4 * rank]
        kept = jnp.where(rows < high_edge, f0, f1)
        fac[...] = jnp.where(rows < low_edge, fac[...], kept)
        return carry

    lax.fori_loop(0, pairs, pair_step, 0)
    half = fac.shape[0] // 2
    f_ref[...] = jnp.concatenate([fac[0:half, :], fac[half : 2 * half, :]], axis=1)


def project_slabs(ids, diff, bases_t):
    rows, width = diff.shape
    mats, rank, _ = bases_t.shape
    hbm = pl.BlockSpec(memory_space=pltpu.HBM)
    vmem = pl.BlockSpec(memory_space=pltpu.VMEM)
    return pl.pallas_call(
        project_kernel,
        out_shape=(
            jax.ShapeDtypeStruct((rows // 2, 2 * rank), jnp.float32),
            jax.ShapeDtypeStruct((mats + mats % 2, 2 * rank, width), jnp.bfloat16),
        ),
        in_specs=[hbm, hbm, hbm],
        out_specs=(vmem, vmem),
        scratch_shapes=[
            pltpu.SMEM(ids.shape, jnp.int32),
            pltpu.VMEM((rows, width), jnp.float32),
            pltpu.VMEM((2, rank, width), jnp.float32),
            pltpu.VMEM((rows, rank), jnp.float32),
            pltpu.SemaphoreType.DMA,
            pltpu.SemaphoreType.DMA,
            pltpu.SemaphoreType.DMA((2,)),
        ],
        compiler_params=pltpu.CompilerParams(vmem_limit_bytes=VMEM_LIMIT),
        cost_estimate=pl.CostEstimate(
            flops=6 * rows * width * rank, bytes_accessed=6 << 20, transcendentals=0
        ),
        name="project_slabs",
    )(
        pltpu.with_memory_space_constraint(ids, pltpu.HBM),
        pltpu.with_memory_space_constraint(diff, pltpu.HBM),
        pltpu.with_memory_space_constraint(bases_t, pltpu.HBM),
    )


def count_ranks(owners_ref, count_ref, base, blocks, visit):
    for n in range(count_ref.shape[0]):
        count_ref[n] = 0
    for k in range(blocks):
        owner = owners_ref[0, base + k]
        rank = count_ref[owner]
        count_ref[owner] = rank + 1
        visit(k, owner, rank)


def pack_kernel(owners_ref, mine_ref, other_ref, mom_ref, out_ref, avg_ref, count_ref):
    n_own, _, lanes = out_ref.shape
    rank = lanes // 2
    blocks = avg_ref.shape[0] // 8
    base = lax.axis_index("own") * blocks
    average = (mine_ref[...] + other_ref[...]) * 0.5
    half = average.shape[0]
    avg_ref[0:half, :] = average[:, 0:rank]
    avg_ref[half : 2 * half, :] = average[:, rank : 2 * rank]
    mom = mom_ref[...].reshape(out_ref.shape[0], out_ref.shape[1], rank)
    out_ref[...] = jnp.concatenate([jnp.zeros_like(mom), mom], axis=2)

    def visit(k, owner, slot):
        out_ref[owner, pl.ds(pl.multiple_of(slot * 8, 8), 8), 0:rank] = avg_ref[8 * k : 8 * k + 8, :]

    count_ranks(owners_ref, count_ref, base, blocks, visit)


def pack_factors(owners, mine, other, momentum):
    n_own, peer, br, rank = momentum.shape
    rows = 2 * mine.shape[0]
    vmem = pl.BlockSpec(memory_space=pltpu.VMEM)
    smem = pl.BlockSpec(memory_space=pltpu.SMEM)
    return pl.pallas_call(
        pack_kernel,
        out_shape=(
            jax.ShapeDtypeStruct((n_own, peer * br, 2 * rank), jnp.float32),
            jax.ShapeDtypeStruct((rows, rank), jnp.float32),
        ),
        in_specs=[smem, vmem, vmem, vmem],
        out_specs=(vmem, vmem),
        scratch_shapes=[pltpu.SMEM((n_own,), jnp.int32)],
        compiler_params=pltpu.CompilerParams(vmem_limit_bytes=4 << 20),
        name="pack_factors",
    )(owners, mine, other, momentum)


def rebuild_kernel(
    ids_ref, owners_ref, recv_ref, avg_ref, mom_ref, w_ref, split_ref, nm_hbm, out_hbm,
    obuf, nbuf, lhs, gath, count_ref, osem, nsem,
):
    rank = lhs.shape[2] // 2
    blocks = avg_ref.shape[0] // 8
    width = obuf.shape[2]
    base = lax.axis_index("own") * blocks
    first, last = id_span(ids_ref, base, blocks)
    total = last - first + 1

    def o_copy(c):
        return pltpu.make_async_copy(
            obuf.at[c], out_hbm.at[:, pl.ds(c * width, width)], osem.at[c]
        )

    n_copy = pltpu.make_async_copy(nbuf, nm_hbm, nsem)

    def visit(k, owner, slot):
        gath[8 * k : 8 * k + 8, :] = recv_ref[owner, pl.ds(pl.multiple_of(slot * 8, 8), 8), :]

    count_ranks(owners_ref, count_ref, base, blocks, visit)
    placed = avg_ref[...]
    held = decay_rate * gath[:, rank : 2 * rank] + placed
    step = -outer_rate * (placed + decay_rate * held)
    rows = lax.broadcasted_iota(jnp.int32, step.shape, 0)
    for t in range(lhs.shape[0]):

        @pl.when(t < total)
        def _():
            low_edge = 8 * slabs_upto(ids_ref, base, blocks, first + t - 1)
            high_edge = 8 * slabs_upto(ids_ref, base, blocks, first + t)
            chosen = jnp.where((rows >= low_edge) & (rows < high_edge), step, 0.0)
            lhs[t] = jnp.concatenate(split_parts(chosen), axis=1)

    def product(t, c):
        basis = split_ref[t, :, pl.ds(c * width, width)]
        high, low = basis[0:rank], basis[rank : 2 * rank]
        left = lhs[t]
        return jnp.dot(
            jnp.concatenate([left, left], axis=1),
            jnp.concatenate([high, high, low, low], axis=0),
            preferred_element_type=jnp.float32,
        )

    for c in range(CHUNKS):
        obuf[c] = w_ref[:, c * width : (c + 1) * width] + product(0, c)

        def add_matrix(t, carry):
            obuf[c] += product(t, c)
            return carry

        lax.fori_loop(1, total, add_matrix, 0)
        o_copy(c).start()
        if c == 0:
            received = recv_ref[:, :, 0:rank].reshape(mom_ref.shape)
            nbuf[...] = decay_rate * mom_ref[...] + received
            n_copy.start()
    for c in range(CHUNKS):
        o_copy(c).wait()
    n_copy.wait()


def rebuild_slabs(ids, owners, received, average, momentum, weights, split):
    rows, width = weights.shape
    mats, lanes, _ = split.shape
    n_own = momentum.shape[0]
    chunk = width // CHUNKS
    vmem = pl.BlockSpec(memory_space=pltpu.VMEM)
    smem = pl.BlockSpec(memory_space=pltpu.SMEM)
    hbm = pl.BlockSpec(memory_space=pltpu.HBM)
    return pl.pallas_call(
        rebuild_kernel,
        out_shape=(
            jax.ShapeDtypeStruct(momentum.shape, jnp.float32),
            jax.ShapeDtypeStruct(weights.shape, jnp.float32),
        ),
        in_specs=[smem, smem, vmem, vmem, vmem, vmem, vmem],
        out_specs=(hbm, hbm),
        scratch_shapes=[
            pltpu.VMEM((CHUNKS, rows, chunk), jnp.float32),
            pltpu.VMEM(momentum.shape, jnp.float32),
            pltpu.VMEM((mats, rows, lanes), jnp.bfloat16),
            pltpu.VMEM((rows, lanes), jnp.float32),
            pltpu.SMEM((n_own,), jnp.int32),
            pltpu.SemaphoreType.DMA((CHUNKS,)),
            pltpu.SemaphoreType.DMA,
        ],
        compiler_params=pltpu.CompilerParams(vmem_limit_bytes=VMEM_LIMIT),
        cost_estimate=pl.CostEstimate(
            flops=8 * rows * width * lanes, bytes_accessed=8 << 20, transcendentals=0
        ),
        name="rebuild_slabs",
    )(ids, owners, received, average, momentum, weights, split)


def per_device(weights, differences, bases, momentum, owners, matrix_ids):
    blocks, br, width = weights.shape
    n_rep = lax.axis_size("rep")
    bases_t = jnp.swapaxes(bases, 1, 2)
    owner_row = owners.T
    mine, split = project_slabs(matrix_ids, differences.reshape(blocks * br, width), bases_t)
    other = lax.ppermute(mine, "rep", [(i, n_rep - 1 - i) for i in range(n_rep)])
    packed, average = pack_factors(owner_row, mine, other, momentum[0])
    received = lax.all_to_all(packed, "own", split_axis=0, concat_axis=0, tiled=True)
    new_momentum, new_weights = rebuild_slabs(
        matrix_ids, owner_row, received, average, momentum[0],
        weights.reshape(blocks * br, width), split,
    )
    return (new_weights.reshape(weights.shape), new_momentum[None])


def solution(mesh):
    placed = (
        P("own", None, None),
        P("rep", "own", None, None),
        P(),
        P("own", None, None, None, None),
        P(),
        P(),
    )
    return jax.shard_map(
        per_device,
        mesh=mesh,
        in_specs=placed,
        out_specs=(P("own", None, None), P("own", None, None, None, None)),
        check_vma=False,
    )
```

```python
import jax
import jax.numpy as jnp
from jax import lax
from jax.experimental import pallas as pl
from jax.experimental.pallas import tpu as pltpu
from jax.sharding import PartitionSpec as P

outer_rate = 0.7
decay_rate = 0.9
CHUNKS = 4
VMEM_LIMIT = 20 << 20
BR = 8


def split_parts(value):
    high = value.astype(jnp.bfloat16)
    low = (value - high.astype(jnp.float32)).astype(jnp.bfloat16)
    return high, low


def dot_nt(a, b):
    return lax.dot_general(a, b, (((1,), (1,)), ((), ())), preferred_element_type=jnp.float32)


def upper_half(shape):
    return lax.broadcasted_iota(jnp.int32, shape, len(shape) - 1) >= shape[-1] // 2


def send_plan(peer):
    pairs = (peer + 1) // 2
    return pairs, (pairs + 1) // 2


def scan_slabs(ids_ref, owners_ref, count_ref, edge_ref, base, blocks, visit):
    for n in range(count_ref.shape[0]):
        count_ref[n] = 0
    first = ids_ref[base]
    edge_ref[0] = 0
    for k in range(blocks):
        edge_ref[ids_ref[base + k] - first + 1] = k + 1
        owner = owners_ref[0, base + k]
        rank = count_ref[owner]
        count_ref[owner] = rank + 1
        visit(k, owner, rank)
    return first, ids_ref[base + blocks - 1]


def project_kernel(
    ids_hbm, owners_hbm, x_hbm, b_hbm, mom_hbm, f_ref, send_ref, split_ref,
    ids_ref, owners_ref, owner_of, rank_of, count_ref, edge_ref,
    xbuf, bbuf, mbuf, fac, isem, osem, xsem, bsem, msem,
):
    blocks = x_hbm.shape[0] // BR
    lanes = send_ref.shape[2]
    rank = lanes // 2
    n_own, peer = mom_hbm.shape[:2]
    pairs, share = send_plan(peer)
    base = lax.axis_index("own") * blocks
    ids_copy = pltpu.make_async_copy(ids_hbm, ids_ref, isem)
    owners_copy = pltpu.make_async_copy(owners_hbm, owners_ref, osem)
    x_copy = pltpu.make_async_copy(x_hbm, xbuf, xsem)
    m_copy = pltpu.make_async_copy(mom_hbm, mbuf.at[:, 0:peer], msem)
    ids_copy.start()
    owners_copy.start()
    x_copy.start()

    def b_copy(index, t):
        return pltpu.make_async_copy(b_hbm.at[index], bbuf.at[t], bsem.at[t])

    ids_copy.wait()
    first = ids_ref[base]
    last = ids_ref[base + blocks - 1]
    b_copy(first, 0).start()
    b_copy(jnp.minimum(first + 1, last), 1).start()
    m_copy.start()
    owners_copy.wait()

    def visit(k, owner, slot):
        owner_of[k] = owner
        rank_of[k] = slot

    scan_slabs(ids_ref, owners_ref, count_ref, edge_ref, base, blocks, visit)
    send_ref[:, 0 : BR * pairs, :] = jnp.zeros((n_own, BR * pairs, lanes), jnp.float32)
    if peer % 2:
        mbuf[:, peer] = jnp.zeros((n_own, BR, rank), jnp.float32)
    m_copy.wait()
    start = lax.axis_index("rep") * (pairs - share)
    for i in range(share):
        slot = 2 * (start + i)
        send_ref[:, BR * (pairs + i) : BR * (pairs + i + 1), :] = jnp.concatenate(
            [mbuf[:, slot], mbuf[:, slot + 1]], axis=2
        )
    x_copy.wait()
    rows = lax.broadcasted_iota(jnp.int32, fac.shape, 0)

    def pair_step(p, carry):
        m0 = first + 2 * p
        m1 = jnp.minimum(m0 + 1, last)

        @pl.when(p > 0)
        def _():
            b_copy(m0, 0).start()
            b_copy(m1, 1).start()

        b_copy(m0, 0).wait()
        b_copy(m1, 1).wait()
        first_basis = jnp.concatenate(split_parts(bbuf[0]), axis=0)
        second_basis = jnp.concatenate(split_parts(bbuf[1]), axis=0)
        split_ref[2 * p] = first_basis
        split_ref[2 * p + 1] = second_basis
        basis = jnp.concatenate([first_basis, second_basis], axis=0)
        high, low = split_parts(xbuf[...])
        total = 0.5 * (dot_nt(high, basis) + dot_nt(low, basis))
        both = []
        for part in (total[:, 0:lanes], total[:, lanes : 2 * lanes]):
            both.append(part + pltpu.roll(part, rank, 1))
        kept = jnp.where(rows < BR * edge_ref[2 * p + 1], both[0], both[1])
        fac[...] = jnp.where(rows < BR * edge_ref[2 * p], fac[...], kept)
        return carry

    lax.fori_loop(0, (last - first + 2) // 2, pair_step, 0)
    half = fac.shape[0] // 2
    f_ref[...] = jnp.where(
        upper_half(f_ref.shape), fac[half : 2 * half, :], fac[0:half, :]
    )
    upper = upper_half((BR, lanes)).astype(jnp.int32)
    for k in range(blocks):
        slot = rank_of[k]
        place = pl.ds(pl.multiple_of(lax.shift_right_logical(slot, 1) * BR, BR), BR)
        tile = send_ref[owner_of[k], place, :]
        mine = upper == lax.bitwise_and(slot, 1)
        send_ref[owner_of[k], place, :] = jnp.where(mine, fac[BR * k : BR * (k + 1), :], tile)


def project_slabs(ids, owners, diff, bases_t, momentum):
    rows, width = diff.shape
    mats, rank, _ = bases_t.shape
    n_own, peer = momentum.shape[:2]
    pairs, share = send_plan(peer)
    blocks = rows // BR
    hbm = pl.BlockSpec(memory_space=pltpu.HBM)
    vmem = pl.BlockSpec(memory_space=pltpu.VMEM)
    return pl.pallas_call(
        project_kernel,
        out_shape=(
            jax.ShapeDtypeStruct((rows // 2, 2 * rank), jnp.float32),
            jax.ShapeDtypeStruct((n_own, BR * (pairs + share), 2 * rank), jnp.float32),
            jax.ShapeDtypeStruct((mats + mats % 2, 2 * rank, width), jnp.bfloat16),
        ),
        in_specs=[hbm] * 5,
        out_specs=(vmem, vmem, vmem),
        scratch_shapes=[
            pltpu.SMEM(ids.shape, jnp.int32),
            pltpu.SMEM(owners.shape, jnp.int32),
            pltpu.SMEM((blocks,), jnp.int32),
            pltpu.SMEM((blocks,), jnp.int32),
            pltpu.SMEM((n_own,), jnp.int32),
            pltpu.SMEM((mats + 2,), jnp.int32),
            pltpu.VMEM((rows, width), jnp.float32),
            pltpu.VMEM((2, rank, width), jnp.float32),
            pltpu.VMEM((n_own, 2 * pairs, BR, rank), jnp.float32),
            pltpu.VMEM((rows, 2 * rank), jnp.float32),
            pltpu.SemaphoreType.DMA,
            pltpu.SemaphoreType.DMA,
            pltpu.SemaphoreType.DMA,
            pltpu.SemaphoreType.DMA((2,)),
            pltpu.SemaphoreType.DMA,
        ],
        compiler_params=pltpu.CompilerParams(vmem_limit_bytes=VMEM_LIMIT),
        cost_estimate=pl.CostEstimate(
            flops=6 * rows * width * rank, bytes_accessed=6 << 20, transcendentals=0
        ),
        name="project_slabs",
    )(*[pltpu.with_memory_space_constraint(v, pltpu.HBM) for v in (ids, owners, diff, bases_t, momentum)])


def rebuild_kernel(
    ids_ref, owners_ref, fmine_ref, fother_ref, mine_ref, other_ref, mom_ref, w_ref, split_ref,
    nm_hbm, out_hbm, obuf, nbuf, sent, lhs, gath, count_ref, edge_ref, osem, nsem,
):
    lanes = gath.shape[1]
    rank = lanes // 2
    blocks = gath.shape[0] // BR
    width = obuf.shape[2]
    n_own, peer = mom_ref.shape[:2]
    pairs, share = send_plan(peer)
    base = lax.axis_index("own") * blocks
    rep = lax.axis_index("rep")

    def o_copy(c):
        return pltpu.make_async_copy(
            obuf.at[c], out_hbm.at[:, pl.ds(c * width, width)], osem.at[c]
        )

    n_copy = pltpu.make_async_copy(nbuf, nm_hbm, nsem)
    sent[rep] = mine_ref[:, BR * pairs : BR * (pairs + share), :]
    sent[1 - rep] = other_ref[:, BR * pairs : BR * (pairs + share), :]
    upper = upper_half((BR, lanes)).astype(jnp.int32)

    def visit(k, owner, slot):
        pair = lax.shift_right_logical(slot, 1)
        source = jnp.where(pair < share, 0, 1)
        row = BR * (pair - source * (pairs - share))
        tile = sent[source, owner, pl.ds(pl.multiple_of(row, BR), BR), :]
        gath[BR * k : BR * (k + 1), :] = jnp.where(upper == lax.bitwise_and(slot, 1), tile, 0.0)

    first, last = scan_slabs(ids_ref, owners_ref, count_ref, edge_ref, base, blocks, visit)
    total = last - first + 1
    average = fmine_ref[...] + fother_ref[...]
    turned = pltpu.roll(average, rank, 1)
    above = upper_half(average.shape)
    placed = jnp.concatenate(
        [jnp.where(above, turned, average), jnp.where(above, average, turned)], axis=0
    )
    picked = gath[...]
    held = decay_rate * (picked + pltpu.roll(picked, rank, 1)) + placed
    step = -outer_rate * (placed + decay_rate * held)
    high = step.astype(jnp.bfloat16).astype(jnp.float32)
    parts = jnp.where(upper_half(step.shape), step - high, high)
    rows = lax.broadcasted_iota(jnp.int32, step.shape, 0)
    for t in range(lhs.shape[0]):

        @pl.when(t < total)
        def _():
            inside = (rows >= BR * edge_ref[t]) & (rows < BR * edge_ref[t + 1])
            lhs[t] = jnp.where(inside, parts, 0.0).astype(jnp.bfloat16)

    def product(t, c):
        basis = split_ref[t, :, pl.ds(c * width, width)]
        top, bottom = basis[0:rank], basis[rank : 2 * rank]
        left = lhs[t]
        return jnp.dot(
            jnp.concatenate([left, left], axis=1),
            jnp.concatenate([top, top, bottom, bottom], axis=0),
            preferred_element_type=jnp.float32,
        )

    for c in range(CHUNKS):
        obuf[c] = w_ref[:, c * width : (c + 1) * width] + product(0, c)

        def add_matrix(t, carry):
            obuf[c] += product(t, c)
            return carry

        lax.fori_loop(1, total, add_matrix, 0)
        o_copy(c).start()
        if c == 0:
            arrived = mine_ref[:, 0 : BR * pairs, :] + other_ref[:, 0 : BR * pairs, :]
            for s in range(peer):
                block = arrived[:, BR * (s // 2) : BR * (s // 2 + 1), :]
                lane = rank * (s % 2)
                nbuf[:, s] = decay_rate * mom_ref[:, s] + block[:, :, lane : lane + rank]
            n_copy.start()
    for c in range(CHUNKS):
        o_copy(c).wait()
    n_copy.wait()


def rebuild_slabs(ids, owners, fmine, fother, mine, other, momentum, weights, split):
    rows, width = weights.shape
    mats, lanes, _ = split.shape
    n_own, peer = momentum.shape[:2]
    _, share = send_plan(peer)
    chunk = width // CHUNKS
    vmem = pl.BlockSpec(memory_space=pltpu.VMEM)
    smem = pl.BlockSpec(memory_space=pltpu.SMEM)
    hbm = pl.BlockSpec(memory_space=pltpu.HBM)
    return pl.pallas_call(
        rebuild_kernel,
        out_shape=(
            jax.ShapeDtypeStruct(momentum.shape, jnp.float32),
            jax.ShapeDtypeStruct(weights.shape, jnp.float32),
        ),
        in_specs=[smem, smem] + [vmem] * 7,
        out_specs=(hbm, hbm),
        scratch_shapes=[
            pltpu.VMEM((CHUNKS, rows, chunk), jnp.float32),
            pltpu.VMEM(momentum.shape, jnp.float32),
            pltpu.VMEM((2, n_own, BR * share, lanes), jnp.float32),
            pltpu.VMEM((mats, rows, lanes), jnp.bfloat16),
            pltpu.VMEM((rows, lanes), jnp.float32),
            pltpu.SMEM((n_own,), jnp.int32),
            pltpu.SMEM((mats + 2,), jnp.int32),
            pltpu.SemaphoreType.DMA((CHUNKS,)),
            pltpu.SemaphoreType.DMA,
        ],
        compiler_params=pltpu.CompilerParams(vmem_limit_bytes=VMEM_LIMIT),
        cost_estimate=pl.CostEstimate(
            flops=8 * rows * width * lanes, bytes_accessed=8 << 20, transcendentals=0
        ),
        name="rebuild_slabs",
    )(ids, owners, fmine, fother, mine, other, momentum, weights, split)


def per_device(weights, differences, bases, momentum, owners, matrix_ids):
    blocks, br, width = weights.shape
    swap = [(0, 1), (1, 0)]
    bases_t = jnp.swapaxes(bases, 1, 2)
    owner_row = owners.T
    fmine, packed, split = project_slabs(
        matrix_ids, owner_row, differences.reshape(blocks * br, width), bases_t, momentum[0]
    )
    fother = lax.ppermute(fmine, "rep", swap)
    mine = lax.all_to_all(packed, "own", split_axis=0, concat_axis=0, tiled=True)
    other = lax.ppermute(mine, "rep", swap)
    new_momentum, new_weights = rebuild_slabs(
        matrix_ids, owner_row, fmine, fother, mine, other, momentum[0],
        weights.reshape(blocks * br, width), split,
    )
    return (new_weights.reshape(weights.shape), new_momentum[None])


def solution(mesh):
    placed = (
        P("own", None, None),
        P("rep", "own", None, None),
        P(),
        P("own", None, None, None, None),
        P(),
        P(),
    )
    return jax.shard_map(
        per_device,
        mesh=mesh,
        in_specs=placed,
        out_specs=(P("own", None, None), P("own", None, None, None, None)),
        check_vma=False,
    )
```

```python
import jax
import jax.numpy as jnp
from jax import lax
from jax.experimental import pallas as pl
from jax.experimental.pallas import tpu as pltpu
from jax.sharding import PartitionSpec as P

outer_rate = 0.7
decay_rate = 0.9
COLUMNS = (0, 1024, 2048, 3072, 4096)
VMEM_LIMIT = 20 << 20
BR = 8


def split_parts(value):
    high = value.astype(jnp.bfloat16)
    low = (value - high.astype(jnp.float32)).astype(jnp.bfloat16)
    return high, low


def dot_nt(a, b):
    return lax.dot_general(a, b, (((1,), (1,)), ((), ())), preferred_element_type=jnp.float32)


def upper_half(shape):
    return lax.broadcasted_iota(jnp.int32, shape, len(shape) - 1) >= shape[-1] // 2


def send_plan(peer):
    pairs = (peer + 1) // 2
    return pairs, (pairs + 1) // 2


def meta_size(blocks, mats):
    return -(-(blocks + mats + 4) // 128) * 128


def project_kernel(
    ids_hbm, owners_hbm, x_hbm, b_hbm, mom_hbm, f_ref, send_ref, split_ref, meta_hbm,
    ids_ref, owners_ref, owner_of, rank_of, count_ref, meta_ref,
    xbuf, bbuf, mbuf, fac, isem, osem, xsem, bsem, msem, tsem,
):
    blocks = x_hbm.shape[0] // BR
    lanes = send_ref.shape[2]
    rank = lanes // 2
    n_own, peer = mom_hbm.shape[:2]
    pairs, share = send_plan(peer)
    base = lax.axis_index("own") * blocks
    ids_copy = pltpu.make_async_copy(ids_hbm, ids_ref, isem)
    owners_copy = pltpu.make_async_copy(owners_hbm, owners_ref, osem)
    x_copy = pltpu.make_async_copy(x_hbm, xbuf, xsem)
    m_copy = pltpu.make_async_copy(mom_hbm, mbuf.at[:, 0:peer], msem)
    ids_copy.start()
    owners_copy.start()
    x_copy.start()

    def b_copy(index, t):
        return pltpu.make_async_copy(b_hbm.at[index], bbuf.at[t], bsem.at[t])

    ids_copy.wait()
    first = ids_ref[base]
    last = ids_ref[base + blocks - 1]
    b_copy(first, 0).start()
    b_copy(jnp.minimum(first + 1, last), 1).start()
    m_copy.start()
    owners_copy.wait()

    for n in range(n_own):
        count_ref[n] = 0
    edge = blocks + 1
    meta_ref[blocks] = last - first + 1
    meta_ref[edge] = 0
    meta_ref[edge + 2] = blocks
    for k in range(blocks):
        meta_ref[edge + ids_ref[base + k] - first + 1] = k + 1
        owner = owners_ref[0, base + k]
        slot = count_ref[owner]
        count_ref[owner] = slot + 1
        owner_of[k] = owner
        rank_of[k] = slot
        pair = lax.shift_right_logical(slot, 1)
        source = jnp.where(pair < share, 0, 1)
        block = (source * n_own + owner) * share + pair - source * (pairs - share)
        meta_ref[k] = BR * block + lax.bitwise_and(slot, 1)
    meta_copy = pltpu.make_async_copy(meta_ref, meta_hbm, tsem)
    meta_copy.start()
    send_ref[:, 0 : BR * pairs, :] = jnp.zeros((n_own, BR * pairs, lanes), jnp.float32)
    if peer % 2:
        mbuf[:, peer] = jnp.zeros((n_own, BR, rank), jnp.float32)
    m_copy.wait()
    start = lax.axis_index("rep") * (pairs - share)
    for i in range(share):
        slot = 2 * (start + i)
        send_ref[:, BR * (pairs + i) : BR * (pairs + i + 1), :] = jnp.concatenate(
            [mbuf[:, slot], mbuf[:, slot + 1]], axis=2
        )
    x_copy.wait()
    rows = lax.broadcasted_iota(jnp.int32, fac.shape, 0)

    def pair_step(p, carry):
        m0 = first + 2 * p
        m1 = jnp.minimum(m0 + 1, last)

        @pl.when(p > 0)
        def _():
            b_copy(m0, 0).start()
            b_copy(m1, 1).start()

        b_copy(m0, 0).wait()
        b_copy(m1, 1).wait()
        first_basis = jnp.concatenate(split_parts(bbuf[0]), axis=0)
        second_basis = jnp.concatenate(split_parts(bbuf[1]), axis=0)
        split_ref[2 * p] = first_basis
        split_ref[2 * p + 1] = second_basis
        basis = jnp.concatenate([first_basis, second_basis], axis=0)
        high, low = split_parts(xbuf[...])
        total = 0.5 * (dot_nt(high, basis) + dot_nt(low, basis))
        both = []
        for part in (total[:, 0:lanes], total[:, lanes : 2 * lanes]):
            both.append(part + pltpu.roll(part, rank, 1))
        kept = jnp.where(rows < BR * meta_ref[edge + 2 * p + 1], both[0], both[1])
        fac[...] = jnp.where(rows < BR * meta_ref[edge + 2 * p], fac[...], kept)
        return carry

    lax.fori_loop(0, (last - first + 2) // 2, pair_step, 0)
    half = fac.shape[0] // 2
    f_ref[...] = jnp.where(
        upper_half(f_ref.shape), fac[half : 2 * half, :], fac[0:half, :]
    )
    upper = upper_half((BR, lanes)).astype(jnp.int32)
    for k in range(blocks):
        slot = rank_of[k]
        place = pl.ds(pl.multiple_of(lax.shift_right_logical(slot, 1) * BR, BR), BR)
        tile = send_ref[owner_of[k], place, :]
        mine = upper == lax.bitwise_and(slot, 1)
        send_ref[owner_of[k], place, :] = jnp.where(mine, fac[BR * k : BR * (k + 1), :], tile)
    meta_copy.wait()


def project_slabs(ids, owners, diff, bases_t, momentum):
    rows, width = diff.shape
    mats, rank, _ = bases_t.shape
    n_own, peer = momentum.shape[:2]
    pairs, share = send_plan(peer)
    blocks = rows // BR
    hbm = pl.BlockSpec(memory_space=pltpu.HBM)
    vmem = pl.BlockSpec(memory_space=pltpu.VMEM)
    return pl.pallas_call(
        project_kernel,
        out_shape=(
            jax.ShapeDtypeStruct((rows // 2, 2 * rank), jnp.float32),
            jax.ShapeDtypeStruct((n_own, BR * (pairs + share), 2 * rank), jnp.float32),
            jax.ShapeDtypeStruct((mats + mats % 2, 2 * rank, width), jnp.bfloat16),
            jax.ShapeDtypeStruct((meta_size(blocks, mats),), jnp.int32),
        ),
        in_specs=[hbm] * 5,
        out_specs=(vmem, vmem, vmem, hbm),
        scratch_shapes=[
            pltpu.SMEM(ids.shape, jnp.int32),
            pltpu.SMEM(owners.shape, jnp.int32),
            pltpu.SMEM((blocks,), jnp.int32),
            pltpu.SMEM((blocks,), jnp.int32),
            pltpu.SMEM((n_own,), jnp.int32),
            pltpu.SMEM((meta_size(blocks, mats),), jnp.int32),
            pltpu.VMEM((rows, width), jnp.float32),
            pltpu.VMEM((2, rank, width), jnp.float32),
            pltpu.VMEM((n_own, 2 * pairs, BR, rank), jnp.float32),
            pltpu.VMEM((rows, 2 * rank), jnp.float32),
            pltpu.SemaphoreType.DMA,
            pltpu.SemaphoreType.DMA,
            pltpu.SemaphoreType.DMA,
            pltpu.SemaphoreType.DMA((2,)),
            pltpu.SemaphoreType.DMA,
            pltpu.SemaphoreType.DMA,
        ],
        compiler_params=pltpu.CompilerParams(vmem_limit_bytes=VMEM_LIMIT),
        cost_estimate=pl.CostEstimate(
            flops=6 * rows * width * rank, bytes_accessed=6 << 20, transcendentals=0
        ),
        name="project_slabs",
    )(*[pltpu.with_memory_space_constraint(v, pltpu.HBM) for v in (ids, owners, diff, bases_t, momentum)])


def rebuild_kernel(
    meta_hbm, fmine_ref, fother_ref, mine_ref, other_ref, mom_ref, w_ref, split_ref,
    nm_hbm, out_hbm, meta_ref, obuf, nbuf, sent, lhs, gath, tsem, osem, nsem,
):
    lanes = gath.shape[1]
    rank = lanes // 2
    blocks = gath.shape[0] // BR
    n_own, peer = mom_ref.shape[:2]
    pairs, share = send_plan(peer)
    edge = blocks + 1
    rep = lax.axis_index("rep")
    meta_copy = pltpu.make_async_copy(meta_hbm, meta_ref, tsem)
    meta_copy.start()

    def o_copy(c):
        cols = pl.ds(COLUMNS[c], COLUMNS[c + 1] - COLUMNS[c])
        return pltpu.make_async_copy(obuf.at[:, cols], out_hbm.at[:, cols], osem.at[c])

    n_copy = pltpu.make_async_copy(nbuf, nm_hbm, nsem)
    span = n_own * BR * share
    for source, ref in ((rep, mine_ref), (1 - rep, other_ref)):
        place = pl.ds(pl.multiple_of(source * span, BR), span)
        sent[place, :] = ref[:, BR * pairs : BR * (pairs + share), :].reshape(span, lanes)
    arrived = mine_ref[:, 0 : BR * pairs, :] + other_ref[:, 0 : BR * pairs, :]
    for s in range(peer):
        block = arrived[:, BR * (s // 2) : BR * (s // 2 + 1), :]
        lane = rank * (s % 2)
        nbuf[:, s] = decay_rate * mom_ref[:, s] + block[:, :, lane : lane + rank]
    n_copy.start()
    average = fmine_ref[...] + fother_ref[...]
    turned = pltpu.roll(average, rank, 1)
    above = upper_half(average.shape)
    placed = jnp.concatenate(
        [jnp.where(above, turned, average), jnp.where(above, average, turned)], axis=0
    )
    upper = upper_half((BR, lanes)).astype(jnp.int32)
    meta_copy.wait()
    total = meta_ref[blocks]
    for k in range(blocks):
        odd = lax.bitwise_and(meta_ref[k], 1)
        tile = sent[pl.ds(pl.multiple_of(meta_ref[k] - odd, BR), BR), :]
        gath[BR * k : BR * (k + 1), :] = jnp.where(upper == odd, tile, 0.0)
    picked = gath[...]
    held = decay_rate * (picked + pltpu.roll(picked, rank, 1)) + placed
    step = -outer_rate * (placed + decay_rate * held)
    high = step.astype(jnp.bfloat16).astype(jnp.float32)
    parts = jnp.where(upper_half(step.shape), step - high, high)
    rows = lax.broadcasted_iota(jnp.int32, step.shape, 0)

    def left_rows(t):
        inside = (rows >= BR * meta_ref[edge + t]) & (rows < BR * meta_ref[edge + t + 1])
        return jnp.where(inside, parts, 0.0).astype(jnp.bfloat16)

    left0 = left_rows(0)
    left1 = left_rows(1)
    lhs[0] = left0
    lhs[1] = left1

    @pl.when(total > 2)
    def _():
        def fill(t, carry):
            lhs[t] = left_rows(t)
            return carry

        lax.fori_loop(2, total, fill, 0)

    def right_rows(t, c):
        start, stop = COLUMNS[c], COLUMNS[c + 1]
        top, bottom = split_ref[t, 0:rank, start:stop], split_ref[t, rank : 2 * rank, start:stop]
        return [top, top, bottom, bottom]

    def product(left, right):
        return jnp.dot(
            jnp.concatenate(left, axis=1),
            jnp.concatenate(right, axis=0),
            preferred_element_type=jnp.float32,
        )

    for c in range(len(COLUMNS) - 1):
        cols = slice(COLUMNS[c], COLUMNS[c + 1])

        @pl.when(total == 1)
        def _():
            one = product([lhs[0], lhs[0]], right_rows(0, c))
            obuf[:, cols] = w_ref[:, cols] + one

        @pl.when(total > 1)
        def _():
            two = product(
                [lhs[0], lhs[0], lhs[1], lhs[1]], right_rows(0, c) + right_rows(1, c)
            )
            obuf[:, cols] = w_ref[:, cols] + two

            def add_matrix(t, carry):
                obuf[:, cols] += product([lhs[t], lhs[t]], right_rows(t, c))
                return carry

            lax.fori_loop(2, total, add_matrix, 0)

        o_copy(c).start()
    for c in range(len(COLUMNS) - 1):
        o_copy(c).wait()
    n_copy.wait()


def rebuild_slabs(meta, fmine, fother, mine, other, momentum, weights, split):
    rows, width = weights.shape
    mats, lanes, _ = split.shape
    n_own, peer = momentum.shape[:2]
    _, share = send_plan(peer)
    vmem = pl.BlockSpec(memory_space=pltpu.VMEM)
    hbm = pl.BlockSpec(memory_space=pltpu.HBM)
    return pl.pallas_call(
        rebuild_kernel,
        out_shape=(
            jax.ShapeDtypeStruct(momentum.shape, jnp.float32),
            jax.ShapeDtypeStruct(weights.shape, jnp.float32),
        ),
        in_specs=[hbm] + [vmem] * 7,
        out_specs=(hbm, hbm),
        scratch_shapes=[
            pltpu.SMEM(meta.shape, jnp.int32),
            pltpu.VMEM((rows, width), jnp.float32),
            pltpu.VMEM(momentum.shape, jnp.float32),
            pltpu.VMEM((2 * n_own * BR * share, lanes), jnp.float32),
            pltpu.VMEM((mats, rows, lanes), jnp.bfloat16),
            pltpu.VMEM((rows, lanes), jnp.float32),
            pltpu.SemaphoreType.DMA,
            pltpu.SemaphoreType.DMA((len(COLUMNS) - 1,)),
            pltpu.SemaphoreType.DMA,
        ],
        compiler_params=pltpu.CompilerParams(vmem_limit_bytes=VMEM_LIMIT),
        cost_estimate=pl.CostEstimate(
            flops=8 * rows * width * lanes, bytes_accessed=8 << 20, transcendentals=0
        ),
        name="rebuild_slabs",
    )(meta, fmine, fother, mine, other, momentum, weights, split)


def per_device(weights, differences, bases, momentum, owners, matrix_ids):
    blocks, br, width = weights.shape
    swap = [(0, 1), (1, 0)]
    bases_t = jnp.swapaxes(bases, 1, 2)
    owner_row = owners.T
    fmine, packed, split, meta = project_slabs(
        matrix_ids, owner_row, differences.reshape(blocks * br, width), bases_t, momentum[0]
    )
    fother = lax.ppermute(fmine, "rep", swap)
    mine = lax.all_to_all(packed, "own", split_axis=0, concat_axis=0, tiled=True)
    other = lax.ppermute(mine, "rep", swap)
    new_momentum, new_weights = rebuild_slabs(
        meta, fmine, fother, mine, other, momentum[0],
        weights.reshape(blocks * br, width), split,
    )
    return (new_weights.reshape(weights.shape), new_momentum[None])


def solution(mesh):
    placed = (
        P("own", None, None),
        P("rep", "own", None, None),
        P(),
        P("own", None, None, None, None),
        P(),
        P(),
    )
    return jax.shard_map(
        per_device,
        mesh=mesh,
        in_specs=placed,
        out_specs=(P("own", None, None), P("own", None, None, None, None)),
        check_vma=False,
    )
```

```python
import jax
import jax.numpy as jnp
from jax import lax
from jax.experimental import pallas as pl
from jax.experimental.pallas import tpu as pltpu
from jax.sharding import PartitionSpec as P

outer_rate = 0.7
decay_rate = 0.9
COLUMNS = (0, 1024, 2048, 3072, 4096)
VMEM_LIMIT = 20 << 20
BR = 8


def split_parts(value):
    high = value.astype(jnp.bfloat16)
    low = (value - high.astype(jnp.float32)).astype(jnp.bfloat16)
    return high, low


def dot_nt(a, b):
    return lax.dot_general(a, b, (((1,), (1,)), ((), ())), preferred_element_type=jnp.float32)


def upper_half(shape):
    return lax.broadcasted_iota(jnp.int32, shape, len(shape) - 1) >= shape[-1] // 2


def send_plan(peer):
    pairs = (peer + 1) // 2
    return pairs, (pairs + 1) // 2


def meta_size(blocks, mats):
    return -(-(blocks + mats + 4) // 8) * 8


def project_kernel(
    ids_hbm, owners_hbm, x_hbm, b_hbm, mom_hbm, f_ref, send_ref, split_ref, table_ref,
    ids_ref, owners_ref, owner_of, rank_of, count_ref, meta_ref,
    xbuf, bbuf, mbuf, fac, isem, osem, xsem, bsem, msem,
):
    blocks = x_hbm.shape[0] // BR
    lanes = send_ref.shape[2]
    rank = lanes // 2
    n_own, peer = mom_hbm.shape[:2]
    pairs, share = send_plan(peer)
    base = lax.axis_index("own") * blocks
    ids_copy = pltpu.make_async_copy(ids_hbm, ids_ref, isem)
    owners_copy = pltpu.make_async_copy(owners_hbm, owners_ref, osem)
    x_copy = pltpu.make_async_copy(x_hbm, xbuf, xsem)
    m_copy = pltpu.make_async_copy(mom_hbm, mbuf.at[:, 0:peer], msem)
    ids_copy.start()
    owners_copy.start()
    x_copy.start()

    def b_copy(index, t):
        return pltpu.make_async_copy(b_hbm.at[index], bbuf.at[t], bsem.at[t])

    ids_copy.wait()
    first = ids_ref[base]
    last = ids_ref[base + blocks - 1]
    b_copy(first, 0).start()
    b_copy(jnp.minimum(first + 1, last), 1).start()
    m_copy.start()
    owners_copy.wait()

    for n in range(n_own):
        count_ref[n] = 0
    edge = blocks + 1
    meta_ref[blocks] = last - first + 1
    meta_ref[edge] = 0
    for n in range(edge + 1, table_ref.shape[0]):
        meta_ref[n] = blocks
    for k in range(blocks):
        meta_ref[edge + ids_ref[base + k] - first + 1] = k + 1
        owner = owners_ref[0, base + k]
        slot = count_ref[owner]
        count_ref[owner] = slot + 1
        owner_of[k] = owner
        rank_of[k] = slot
        pair = lax.shift_right_logical(slot, 1)
        source = jnp.where(pair < share, 0, 1)
        block = (source * n_own + owner) * share + pair - source * (pairs - share)
        meta_ref[k] = BR * block + lax.bitwise_and(slot, 1)
    for n in range(table_ref.shape[0]):
        table_ref[n : n + 1, :] = jnp.full((1, lanes), meta_ref[n], jnp.int32)
    send_ref[:, 0 : BR * pairs, :] = jnp.zeros((n_own, BR * pairs, lanes), jnp.float32)
    if peer % 2:
        mbuf[:, peer] = jnp.zeros((n_own, BR, rank), jnp.float32)
    m_copy.wait()
    start = lax.axis_index("rep") * (pairs - share)
    for i in range(share):
        slot = 2 * (start + i)
        send_ref[:, BR * (pairs + i) : BR * (pairs + i + 1), :] = jnp.concatenate(
            [mbuf[:, slot], mbuf[:, slot + 1]], axis=2
        )
    x_copy.wait()
    rows = lax.broadcasted_iota(jnp.int32, fac.shape, 0)

    def pair_step(p, carry):
        m0 = first + 2 * p
        m1 = jnp.minimum(m0 + 1, last)

        @pl.when(p > 0)
        def _():
            b_copy(m0, 0).start()
            b_copy(m1, 1).start()

        b_copy(m0, 0).wait()
        b_copy(m1, 1).wait()
        first_basis = jnp.concatenate(split_parts(bbuf[0]), axis=0)
        second_basis = jnp.concatenate(split_parts(bbuf[1]), axis=0)
        split_ref[2 * p] = first_basis
        split_ref[2 * p + 1] = second_basis
        basis = jnp.concatenate([first_basis, second_basis], axis=0)
        high, low = split_parts(xbuf[...])
        total = 0.5 * (dot_nt(high, basis) + dot_nt(low, basis))
        both = []
        for part in (total[:, 0:lanes], total[:, lanes : 2 * lanes]):
            both.append(part + pltpu.roll(part, rank, 1))
        kept = jnp.where(rows < BR * meta_ref[edge + 2 * p + 1], both[0], both[1])
        fac[...] = jnp.where(rows < BR * meta_ref[edge + 2 * p], fac[...], kept)
        return carry

    lax.fori_loop(0, (last - first + 2) // 2, pair_step, 0)
    half = fac.shape[0] // 2
    f_ref[...] = jnp.where(
        upper_half(f_ref.shape), fac[half : 2 * half, :], fac[0:half, :]
    )
    upper = upper_half((BR, lanes)).astype(jnp.int32)
    for k in range(blocks):
        slot = rank_of[k]
        place = pl.ds(pl.multiple_of(lax.shift_right_logical(slot, 1) * BR, BR), BR)
        tile = send_ref[owner_of[k], place, :]
        mine = upper == lax.bitwise_and(slot, 1)
        send_ref[owner_of[k], place, :] = jnp.where(mine, fac[BR * k : BR * (k + 1), :], tile)


def project_slabs(ids, owners, diff, bases_t, momentum):
    rows, width = diff.shape
    mats, rank, _ = bases_t.shape
    n_own, peer = momentum.shape[:2]
    pairs, share = send_plan(peer)
    blocks = rows // BR
    hbm = pl.BlockSpec(memory_space=pltpu.HBM)
    vmem = pl.BlockSpec(memory_space=pltpu.VMEM)
    return pl.pallas_call(
        project_kernel,
        out_shape=(
            jax.ShapeDtypeStruct((rows // 2, 2 * rank), jnp.float32),
            jax.ShapeDtypeStruct((n_own, BR * (pairs + share), 2 * rank), jnp.float32),
            jax.ShapeDtypeStruct((mats + mats % 2, 2 * rank, width), jnp.bfloat16),
            jax.ShapeDtypeStruct((meta_size(blocks, mats), 2 * rank), jnp.int32),
        ),
        in_specs=[hbm] * 5,
        out_specs=(vmem,) * 4,
        scratch_shapes=[
            pltpu.SMEM(ids.shape, jnp.int32),
            pltpu.SMEM(owners.shape, jnp.int32),
            pltpu.SMEM((blocks,), jnp.int32),
            pltpu.SMEM((blocks,), jnp.int32),
            pltpu.SMEM((n_own,), jnp.int32),
            pltpu.SMEM((meta_size(blocks, mats),), jnp.int32),
            pltpu.VMEM((rows, width), jnp.float32),
            pltpu.VMEM((2, rank, width), jnp.float32),
            pltpu.VMEM((n_own, 2 * pairs, BR, rank), jnp.float32),
            pltpu.VMEM((rows, 2 * rank), jnp.float32),
            pltpu.SemaphoreType.DMA,
            pltpu.SemaphoreType.DMA,
            pltpu.SemaphoreType.DMA,
            pltpu.SemaphoreType.DMA((2,)),
            pltpu.SemaphoreType.DMA,
        ],
        compiler_params=pltpu.CompilerParams(vmem_limit_bytes=VMEM_LIMIT),
        cost_estimate=pl.CostEstimate(
            flops=6 * rows * width * rank, bytes_accessed=6 << 20, transcendentals=0
        ),
        name="project_slabs",
    )(*[pltpu.with_memory_space_constraint(v, pltpu.HBM) for v in (ids, owners, diff, bases_t, momentum)])


def rebuild_kernel(
    table_ref, fmine_ref, fother_ref, mine_ref, other_ref, mom_ref, w_ref, split_ref,
    nm_hbm, out_hbm, obuf, nbuf, sent, lhs, gath, osem, nsem,
):
    lanes = gath.shape[1]
    rank = lanes // 2
    blocks = gath.shape[0] // BR
    n_own, peer = mom_ref.shape[:2]
    pairs, share = send_plan(peer)
    edge = blocks + 1
    rep = lax.axis_index("rep")

    def o_copy(c):
        cols = pl.ds(COLUMNS[c], COLUMNS[c + 1] - COLUMNS[c])
        return pltpu.make_async_copy(obuf.at[:, cols], out_hbm.at[:, cols], osem.at[c])

    n_copy = pltpu.make_async_copy(nbuf, nm_hbm, nsem)
    span = n_own * BR * share
    for source, ref in ((rep, mine_ref), (1 - rep, other_ref)):
        place = pl.ds(pl.multiple_of(source * span, BR), span)
        sent[place, :] = ref[:, BR * pairs : BR * (pairs + share), :].reshape(span, lanes)
    arrived = mine_ref[:, 0 : BR * pairs, :] + other_ref[:, 0 : BR * pairs, :]
    for s in range(peer):
        block = arrived[:, BR * (s // 2) : BR * (s // 2 + 1), :]
        lane = rank * (s % 2)
        nbuf[:, s] = decay_rate * mom_ref[:, s] + block[:, :, lane : lane + rank]
    n_copy.start()
    average = fmine_ref[...] + fother_ref[...]
    turned = pltpu.roll(average, rank, 1)
    above = upper_half(average.shape)
    placed = jnp.concatenate(
        [jnp.where(above, turned, average), jnp.where(above, average, turned)], axis=0
    )
    upper = upper_half((BR, lanes)).astype(jnp.int32)
    total = table_ref[blocks : blocks + 1, 0:1][0, 0]
    for k in range(blocks):
        odd = lax.bitwise_and(table_ref[k : k + 1, :], 1)
        row = lax.bitwise_and(table_ref[k : k + 1, 0:1][0, 0], -BR)
        tile = sent[pl.ds(pl.multiple_of(row, BR), BR), :]
        gath[BR * k : BR * (k + 1), :] = jnp.where(upper == odd, tile, 0.0)
    picked = gath[...]
    held = decay_rate * (picked + pltpu.roll(picked, rank, 1)) + placed
    step = -outer_rate * (placed + decay_rate * held)
    high = step.astype(jnp.bfloat16).astype(jnp.float32)
    parts = jnp.where(upper_half(step.shape), step - high, high)
    rows = lax.broadcasted_iota(jnp.int32, step.shape, 0)

    def left_rows(t):
        start = BR * table_ref[pl.ds(edge + t, 1), :]
        stop = BR * table_ref[pl.ds(edge + t + 1, 1), :]
        inside = (rows >= start) & (rows < stop)
        return jnp.where(inside, parts, 0.0).astype(jnp.bfloat16)

    left0 = left_rows(0)
    left1 = left_rows(1)
    lhs[0] = left0
    lhs[1] = left1

    @pl.when(total > 2)
    def _():
        def fill(t, carry):
            lhs[t] = left_rows(t)
            return carry

        lax.fori_loop(2, total, fill, 0)

    def right_rows(t, c):
        start, stop = COLUMNS[c], COLUMNS[c + 1]
        top, bottom = split_ref[t, 0:rank, start:stop], split_ref[t, rank : 2 * rank, start:stop]
        return [top, top, bottom, bottom]

    def product(left, right):
        return jnp.dot(
            jnp.concatenate(left, axis=1),
            jnp.concatenate(right, axis=0),
            preferred_element_type=jnp.float32,
        )

    for c in range(len(COLUMNS) - 1):
        cols = slice(COLUMNS[c], COLUMNS[c + 1])

        @pl.when(total == 1)
        def _():
            one = product([lhs[0], lhs[0]], right_rows(0, c))
            obuf[:, cols] = w_ref[:, cols] + one

        @pl.when(total > 1)
        def _():
            two = product(
                [lhs[0], lhs[0], lhs[1], lhs[1]], right_rows(0, c) + right_rows(1, c)
            )
            obuf[:, cols] = w_ref[:, cols] + two

            def add_matrix(t, carry):
                obuf[:, cols] += product([lhs[t], lhs[t]], right_rows(t, c))
                return carry

            lax.fori_loop(2, total, add_matrix, 0)

        o_copy(c).start()
    for c in range(len(COLUMNS) - 1):
        o_copy(c).wait()
    n_copy.wait()


def rebuild_slabs(meta, fmine, fother, mine, other, momentum, weights, split):
    rows, width = weights.shape
    mats, lanes, _ = split.shape
    n_own, peer = momentum.shape[:2]
    _, share = send_plan(peer)
    vmem = pl.BlockSpec(memory_space=pltpu.VMEM)
    hbm = pl.BlockSpec(memory_space=pltpu.HBM)
    return pl.pallas_call(
        rebuild_kernel,
        out_shape=(
            jax.ShapeDtypeStruct(momentum.shape, jnp.float32),
            jax.ShapeDtypeStruct(weights.shape, jnp.float32),
        ),
        in_specs=[vmem] * 8,
        out_specs=(hbm, hbm),
        scratch_shapes=[
            pltpu.VMEM((rows, width), jnp.float32),
            pltpu.VMEM(momentum.shape, jnp.float32),
            pltpu.VMEM((2 * n_own * BR * share, lanes), jnp.float32),
            pltpu.VMEM((mats, rows, lanes), jnp.bfloat16),
            pltpu.VMEM((rows, lanes), jnp.float32),
            pltpu.SemaphoreType.DMA((len(COLUMNS) - 1,)),
            pltpu.SemaphoreType.DMA,
        ],
        compiler_params=pltpu.CompilerParams(vmem_limit_bytes=VMEM_LIMIT),
        cost_estimate=pl.CostEstimate(
            flops=8 * rows * width * lanes, bytes_accessed=8 << 20, transcendentals=0
        ),
        name="rebuild_slabs",
    )(meta, fmine, fother, mine, other, momentum, weights, split)


def per_device(weights, differences, bases, momentum, owners, matrix_ids):
    blocks, br, width = weights.shape
    swap = [(0, 1), (1, 0)]
    bases_t = jnp.swapaxes(bases, 1, 2)
    owner_row = owners.T
    fmine, packed, split, meta = project_slabs(
        matrix_ids, owner_row, differences.reshape(blocks * br, width), bases_t, momentum[0]
    )
    fother = lax.ppermute(fmine, "rep", swap)
    mine = lax.all_to_all(packed, "own", split_axis=0, concat_axis=0, tiled=True)
    other = lax.ppermute(mine, "rep", swap)
    new_momentum, new_weights = rebuild_slabs(
        meta, fmine, fother, mine, other, momentum[0],
        weights.reshape(blocks * br, width), split,
    )
    return (new_weights.reshape(weights.shape), new_momentum[None])


def solution(mesh):
    placed = (
        P("own", None, None),
        P("rep", "own", None, None),
        P(),
        P("own", None, None, None, None),
        P(),
        P(),
    )
    return jax.shard_map(
        per_device,
        mesh=mesh,
        in_specs=placed,
        out_specs=(P("own", None, None), P("own", None, None, None, None)),
        check_vma=False,
    )
```

```python
import jax
import jax.numpy as jnp
from jax import lax
from jax.experimental import pallas as pl
from jax.experimental.pallas import tpu as pltpu
from jax.sharding import PartitionSpec as P

outer_rate = 0.7
decay_rate = 0.9
COLUMNS = (0, 1024, 2048, 3072, 4096)
VMEM_LIMIT = 20 << 20
BR = 8


def split_parts(value):
    high = value.astype(jnp.bfloat16)
    low = (value - high.astype(jnp.float32)).astype(jnp.bfloat16)
    return high, low


def dot_nt(a, b):
    return lax.dot_general(a, b, (((1,), (1,)), ((), ())), preferred_element_type=jnp.float32)


def upper_half(shape):
    return lax.broadcasted_iota(jnp.int32, shape, len(shape) - 1) >= shape[-1] // 2


def send_plan(peer):
    pairs = (peer + 1) // 2
    return pairs, (pairs + 1) // 2


def meta_size(blocks, mats):
    return -(-(blocks + mats + 4) // 8) * 8


def project_kernel(
    ids_hbm, owners_hbm, x_hbm, b_hbm, mom_hbm, f_ref, send_ref, split_ref, table_ref,
    ids_ref, owners_ref, owner_of, rank_of, count_ref, meta_ref,
    xbuf, bbuf, mbuf, fac, isem, osem, xsem, bsem, msem,
):
    blocks = x_hbm.shape[0] // BR
    lanes = send_ref.shape[2]
    rank = lanes // 2
    n_own, peer = mom_hbm.shape[:2]
    pairs, share = send_plan(peer)
    base = lax.axis_index("own") * blocks
    ids_copy = pltpu.make_async_copy(ids_hbm, ids_ref, isem)
    owners_copy = pltpu.make_async_copy(owners_hbm, owners_ref, osem)
    x_copy = pltpu.make_async_copy(x_hbm, xbuf, xsem)
    m_copy = pltpu.make_async_copy(mom_hbm, mbuf.at[:, 0:peer], msem)
    ids_copy.start()
    owners_copy.start()
    x_copy.start()

    def b_copy(index, t):
        return pltpu.make_async_copy(b_hbm.at[index], bbuf.at[t], bsem.at[t])

    ids_copy.wait()
    first = ids_ref[base]
    last = ids_ref[base + blocks - 1]
    b_copy(first, 0).start()

    @pl.when(first < last)
    def _():
        b_copy(first + 1, 1).start()

    m_copy.start()
    owners_copy.wait()

    for n in range(n_own):
        count_ref[n] = 0
    edge = blocks + 1
    meta_ref[blocks] = last - first + 1
    meta_ref[edge] = 0
    for n in range(edge + 1, table_ref.shape[0]):
        meta_ref[n] = blocks
    for k in range(blocks):
        meta_ref[edge + ids_ref[base + k] - first + 1] = k + 1
        owner = owners_ref[0, base + k]
        slot = count_ref[owner]
        count_ref[owner] = slot + 1
        owner_of[k] = owner
        rank_of[k] = slot
        pair = lax.shift_right_logical(slot, 1)
        source = jnp.where(pair < share, 0, 1)
        block = (source * n_own + owner) * share + pair - source * (pairs - share)
        meta_ref[k] = BR * block + lax.bitwise_and(slot, 1)
    for n in range(table_ref.shape[0]):
        table_ref[n : n + 1, :] = jnp.full((1, lanes), meta_ref[n], jnp.int32)
    send_ref[:, 0 : BR * pairs, :] = jnp.zeros((n_own, BR * pairs, lanes), jnp.float32)
    if peer % 2:
        mbuf[:, peer] = jnp.zeros((n_own, BR, rank), jnp.float32)
    m_copy.wait()
    start = lax.axis_index("rep") * (pairs - share)
    for i in range(share):
        slot = 2 * (start + i)
        send_ref[:, BR * (pairs + i) : BR * (pairs + i + 1), :] = jnp.concatenate(
            [mbuf[:, slot], mbuf[:, slot + 1]], axis=2
        )
    x_copy.wait()
    rows = lax.broadcasted_iota(jnp.int32, fac.shape, 0)

    def pair_step(p, carry):
        m0 = first + 2 * p
        paired = m0 < last

        @pl.when(p > 0)
        def _():
            b_copy(m0, 0).start()

        @pl.when((p > 0) & paired)
        def _():
            b_copy(m0 + 1, 1).start()

        b_copy(m0, 0).wait()

        @pl.when(paired)
        def _():
            b_copy(m0 + 1, 1).wait()

        first_basis = jnp.concatenate(split_parts(bbuf[0]), axis=0)
        second_basis = jnp.concatenate(split_parts(bbuf[jnp.where(paired, 1, 0)]), axis=0)
        split_ref[2 * p] = first_basis
        split_ref[2 * p + 1] = second_basis
        basis = jnp.concatenate([first_basis, second_basis], axis=0)
        high, low = split_parts(xbuf[...])
        total = 0.5 * (dot_nt(high, basis) + dot_nt(low, basis))
        both = []
        for part in (total[:, 0:lanes], total[:, lanes : 2 * lanes]):
            both.append(part + pltpu.roll(part, rank, 1))
        kept = jnp.where(rows < BR * meta_ref[edge + 2 * p + 1], both[0], both[1])
        fac[...] = jnp.where(rows < BR * meta_ref[edge + 2 * p], fac[...], kept)
        return carry

    lax.fori_loop(0, (last - first + 2) // 2, pair_step, 0)
    half = fac.shape[0] // 2
    f_ref[...] = jnp.where(
        upper_half(f_ref.shape), fac[half : 2 * half, :], fac[0:half, :]
    )
    upper = upper_half((BR, lanes)).astype(jnp.int32)
    for k in range(blocks):
        slot = rank_of[k]
        place = pl.ds(pl.multiple_of(lax.shift_right_logical(slot, 1) * BR, BR), BR)
        tile = send_ref[owner_of[k], place, :]
        mine = upper == lax.bitwise_and(slot, 1)
        send_ref[owner_of[k], place, :] = jnp.where(mine, fac[BR * k : BR * (k + 1), :], tile)


def project_slabs(ids, owners, diff, bases_t, momentum):
    rows, width = diff.shape
    mats, rank, _ = bases_t.shape
    n_own, peer = momentum.shape[:2]
    pairs, share = send_plan(peer)
    blocks = rows // BR
    hbm = pl.BlockSpec(memory_space=pltpu.HBM)
    vmem = pl.BlockSpec(memory_space=pltpu.VMEM)
    return pl.pallas_call(
        project_kernel,
        out_shape=(
            jax.ShapeDtypeStruct((rows // 2, 2 * rank), jnp.float32),
            jax.ShapeDtypeStruct((n_own, BR * (pairs + share), 2 * rank), jnp.float32),
            jax.ShapeDtypeStruct((mats + mats % 2, 2 * rank, width), jnp.bfloat16),
            jax.ShapeDtypeStruct((meta_size(blocks, mats), 2 * rank), jnp.int32),
        ),
        in_specs=[hbm] * 5,
        out_specs=(vmem,) * 4,
        scratch_shapes=[
            pltpu.SMEM(ids.shape, jnp.int32),
            pltpu.SMEM(owners.shape, jnp.int32),
            pltpu.SMEM((blocks,), jnp.int32),
            pltpu.SMEM((blocks,), jnp.int32),
            pltpu.SMEM((n_own,), jnp.int32),
            pltpu.SMEM((meta_size(blocks, mats),), jnp.int32),
            pltpu.VMEM((rows, width), jnp.float32),
            pltpu.VMEM((2, rank, width), jnp.float32),
            pltpu.VMEM((n_own, 2 * pairs, BR, rank), jnp.float32),
            pltpu.VMEM((rows, 2 * rank), jnp.float32),
            pltpu.SemaphoreType.DMA,
            pltpu.SemaphoreType.DMA,
            pltpu.SemaphoreType.DMA,
            pltpu.SemaphoreType.DMA((2,)),
            pltpu.SemaphoreType.DMA,
        ],
        compiler_params=pltpu.CompilerParams(vmem_limit_bytes=VMEM_LIMIT),
        cost_estimate=pl.CostEstimate(
            flops=6 * rows * width * rank, bytes_accessed=6 << 20, transcendentals=0
        ),
        name="project_slabs",
    )(*[pltpu.with_memory_space_constraint(v, pltpu.HBM) for v in (ids, owners, diff, bases_t, momentum)])


def rebuild_kernel(
    table_ref, fmine_ref, fother_ref, mine_ref, other_ref, mom_ref, w_ref, split_ref,
    nm_hbm, out_hbm, obuf, nbuf, sent, lhs, gath, osem, nsem,
):
    lanes = gath.shape[1]
    rank = lanes // 2
    blocks = gath.shape[0] // BR
    n_own, peer = mom_ref.shape[:2]
    pairs, share = send_plan(peer)
    edge = blocks + 1
    rep = lax.axis_index("rep")

    def o_copy(c):
        cols = pl.ds(COLUMNS[c], COLUMNS[c + 1] - COLUMNS[c])
        return pltpu.make_async_copy(obuf.at[:, cols], out_hbm.at[:, cols], osem.at[c])

    n_copy = pltpu.make_async_copy(nbuf, nm_hbm, nsem)
    span = n_own * BR * share
    for source, ref in ((rep, mine_ref), (1 - rep, other_ref)):
        place = pl.ds(pl.multiple_of(source * span, BR), span)
        sent[place, :] = ref[:, BR * pairs : BR * (pairs + share), :].reshape(span, lanes)
    arrived = mine_ref[:, 0 : BR * pairs, :] + other_ref[:, 0 : BR * pairs, :]
    for s in range(peer):
        block = arrived[:, BR * (s // 2) : BR * (s // 2 + 1), :]
        lane = rank * (s % 2)
        nbuf[:, s] = decay_rate * mom_ref[:, s] + block[:, :, lane : lane + rank]
    n_copy.start()
    average = fmine_ref[...] + fother_ref[...]
    turned = pltpu.roll(average, rank, 1)
    above = upper_half(average.shape)
    placed = jnp.concatenate(
        [jnp.where(above, turned, average), jnp.where(above, average, turned)], axis=0
    )
    upper = upper_half((BR, lanes)).astype(jnp.int32)
    total = table_ref[blocks : blocks + 1, 0:1][0, 0]
    for k in range(blocks):
        odd = lax.bitwise_and(table_ref[k : k + 1, :], 1)
        row = lax.bitwise_and(table_ref[k : k + 1, 0:1][0, 0], -BR)
        tile = sent[pl.ds(pl.multiple_of(row, BR), BR), :]
        gath[BR * k : BR * (k + 1), :] = jnp.where(upper == odd, tile, 0.0)
    picked = gath[...]
    held = decay_rate * (picked + pltpu.roll(picked, rank, 1)) + placed
    step = -outer_rate * (placed + decay_rate * held)
    high = step.astype(jnp.bfloat16).astype(jnp.float32)
    parts = jnp.where(upper_half(step.shape), step - high, high)
    rows = lax.broadcasted_iota(jnp.int32, step.shape, 0)

    def left_rows(t):
        start = BR * table_ref[pl.ds(edge + t, 1), :]
        stop = BR * table_ref[pl.ds(edge + t + 1, 1), :]
        inside = (rows >= start) & (rows < stop)
        return jnp.where(inside, parts, 0.0).astype(jnp.bfloat16)

    left0 = left_rows(0)
    left1 = left_rows(1)
    lhs[0] = left0
    lhs[1] = left1

    @pl.when(total > 2)
    def _():
        def fill(t, carry):
            lhs[t] = left_rows(t)
            return carry

        lax.fori_loop(2, total, fill, 0)

    def right_rows(t, c):
        start, stop = COLUMNS[c], COLUMNS[c + 1]
        top, bottom = split_ref[t, 0:rank, start:stop], split_ref[t, rank : 2 * rank, start:stop]
        return [top, top, bottom, bottom]

    def product(left, right):
        return jnp.dot(
            jnp.concatenate(left, axis=1),
            jnp.concatenate(right, axis=0),
            preferred_element_type=jnp.float32,
        )

    for c in range(len(COLUMNS) - 1):
        cols = slice(COLUMNS[c], COLUMNS[c + 1])

        @pl.when(total == 1)
        def _():
            one = product([lhs[0], lhs[0]], right_rows(0, c))
            obuf[:, cols] = w_ref[:, cols] + one

        @pl.when(total > 1)
        def _():
            two = product(
                [lhs[0], lhs[0], lhs[1], lhs[1]], right_rows(0, c) + right_rows(1, c)
            )
            obuf[:, cols] = w_ref[:, cols] + two

            def add_matrix(t, carry):
                obuf[:, cols] += product([lhs[t], lhs[t]], right_rows(t, c))
                return carry

            lax.fori_loop(2, total, add_matrix, 0)

        o_copy(c).start()
    for c in range(len(COLUMNS) - 1):
        o_copy(c).wait()
    n_copy.wait()


def rebuild_slabs(meta, fmine, fother, mine, other, momentum, weights, split):
    rows, width = weights.shape
    mats, lanes, _ = split.shape
    n_own, peer = momentum.shape[:2]
    _, share = send_plan(peer)
    vmem = pl.BlockSpec(memory_space=pltpu.VMEM)
    hbm = pl.BlockSpec(memory_space=pltpu.HBM)
    return pl.pallas_call(
        rebuild_kernel,
        out_shape=(
            jax.ShapeDtypeStruct(momentum.shape, jnp.float32),
            jax.ShapeDtypeStruct(weights.shape, jnp.float32),
        ),
        in_specs=[vmem] * 8,
        out_specs=(hbm, hbm),
        scratch_shapes=[
            pltpu.VMEM((rows, width), jnp.float32),
            pltpu.VMEM(momentum.shape, jnp.float32),
            pltpu.VMEM((2 * n_own * BR * share, lanes), jnp.float32),
            pltpu.VMEM((mats, rows, lanes), jnp.bfloat16),
            pltpu.VMEM((rows, lanes), jnp.float32),
            pltpu.SemaphoreType.DMA((len(COLUMNS) - 1,)),
            pltpu.SemaphoreType.DMA,
        ],
        compiler_params=pltpu.CompilerParams(vmem_limit_bytes=VMEM_LIMIT),
        cost_estimate=pl.CostEstimate(
            flops=8 * rows * width * lanes, bytes_accessed=8 << 20, transcendentals=0
        ),
        name="rebuild_slabs",
    )(meta, fmine, fother, mine, other, momentum, weights, split)


def per_device(weights, differences, bases, momentum, owners, matrix_ids):
    blocks, br, width = weights.shape
    swap = [(0, 1), (1, 0)]
    bases_t = jnp.swapaxes(bases, 1, 2)
    owner_row = owners.T
    fmine, packed, split, meta = project_slabs(
        matrix_ids, owner_row, differences.reshape(blocks * br, width), bases_t, momentum[0]
    )
    fother = lax.ppermute(fmine, "rep", swap)
    mine = lax.all_to_all(packed, "own", split_axis=0, concat_axis=0, tiled=True)
    other = lax.ppermute(mine, "rep", swap)
    new_momentum, new_weights = rebuild_slabs(
        meta, fmine, fother, mine, other, momentum[0],
        weights.reshape(blocks * br, width), split,
    )
    return (new_weights.reshape(weights.shape), new_momentum[None])


def solution(mesh):
    placed = (
        P("own", None, None),
        P("rep", "own", None, None),
        P(),
        P("own", None, None, None, None),
        P(),
        P(),
    )
    return jax.shard_map(
        per_device,
        mesh=mesh,
        in_specs=placed,
        out_specs=(P("own", None, None), P("own", None, None, None, None)),
        check_vma=False,
    )
```

```python
import jax
import jax.numpy as jnp
from jax import lax
from jax.experimental import pallas as pl
from jax.experimental.pallas import tpu as pltpu
from jax.sharding import PartitionSpec as P

outer_rate = 0.7
decay_rate = 0.9
COLUMNS = (0, 1024, 2048, 3072, 4096)
VMEM_LIMIT = 20 << 20
BR = 8


def split_parts(value):
    high = value.astype(jnp.bfloat16)
    low = (value - high.astype(jnp.float32)).astype(jnp.bfloat16)
    return high, low


def dot_nt(a, b):
    return lax.dot_general(a, b, (((1,), (1,)), ((), ())), preferred_element_type=jnp.float32)


def upper_half(shape):
    return lax.broadcasted_iota(jnp.int32, shape, len(shape) - 1) >= shape[-1] // 2


def send_plan(peer):
    pairs = (peer + 1) // 2
    return pairs, (pairs + 1) // 2


def meta_size(blocks, mats):
    return -(-(blocks + mats + 4) // 8) * 8


def project_kernel(
    ids_hbm, owners_hbm, x_hbm, b_hbm, mom_hbm, f_ref, send_ref, split_ref, table_ref,
    ids_ref, owners_ref, owner_of, rank_of, count_ref, meta_ref,
    xbuf, bbuf, mbuf, fac, isem, osem, xsem, bsem, msem,
):
    blocks = x_hbm.shape[0] // BR
    lanes = send_ref.shape[2]
    rank = lanes // 2
    n_own, peer = mom_hbm.shape[:2]
    pairs, share = send_plan(peer)
    base = lax.axis_index("own") * blocks
    ids_copy = pltpu.make_async_copy(ids_hbm, ids_ref, isem)
    owners_copy = pltpu.make_async_copy(owners_hbm, owners_ref, osem)
    x_copy = pltpu.make_async_copy(x_hbm, xbuf, xsem)
    m_copy = pltpu.make_async_copy(mom_hbm, mbuf.at[:, 0:peer], msem)
    ids_copy.start()
    owners_copy.start()
    x_copy.start()

    def b_copy(index, t):
        return pltpu.make_async_copy(b_hbm.at[index], bbuf.at[t], bsem.at[t])

    ids_copy.wait()
    first = ids_ref[base]
    last = ids_ref[base + blocks - 1]
    b_copy(first, 0).start()

    @pl.when(first < last)
    def _():
        b_copy(first + 1, 1).start()

    m_copy.start()
    owners_copy.wait()

    for n in range(n_own):
        count_ref[n] = 0
    edge = blocks + 1
    meta_ref[blocks] = last - first + 1
    meta_ref[edge] = 0
    for n in range(edge + 1, table_ref.shape[0]):
        meta_ref[n] = blocks
    for k in range(blocks):
        meta_ref[edge + ids_ref[base + k] - first + 1] = k + 1
        owner = owners_ref[0, base + k]
        slot = count_ref[owner]
        count_ref[owner] = slot + 1
        owner_of[k] = owner
        rank_of[k] = slot
        pair = lax.shift_right_logical(slot, 1)
        source = jnp.where(pair < share, 0, 1)
        block = (source * n_own + owner) * share + pair - source * (pairs - share)
        meta_ref[k] = BR * block + lax.bitwise_and(slot, 1)
    for n in range(table_ref.shape[0]):
        table_ref[n : n + 1, :] = jnp.full((1, lanes), meta_ref[n], jnp.int32)
    send_ref[:, 0 : BR * pairs, :] = jnp.zeros((n_own, BR * pairs, lanes), jnp.float32)
    if peer % 2:
        mbuf[:, peer] = jnp.zeros((n_own, BR, rank), jnp.float32)
    m_copy.wait()
    start = lax.axis_index("rep") * (pairs - share)
    for i in range(share):
        slot = 2 * (start + i)
        send_ref[:, BR * (pairs + i) : BR * (pairs + i + 1), :] = jnp.concatenate(
            [mbuf[:, slot], mbuf[:, slot + 1]], axis=2
        )
    x_copy.wait()
    rows = lax.broadcasted_iota(jnp.int32, fac.shape, 0)

    def pair_step(p, carry):
        m0 = first + 2 * p
        paired = m0 < last

        @pl.when(p > 0)
        def _():
            b_copy(m0, 0).start()

        @pl.when((p > 0) & paired)
        def _():
            b_copy(m0 + 1, 1).start()

        b_copy(m0, 0).wait()

        @pl.when(paired)
        def _():
            b_copy(m0 + 1, 1).wait()

        first_basis = jnp.concatenate(split_parts(bbuf[0]), axis=0)
        second_basis = jnp.concatenate(split_parts(bbuf[jnp.where(paired, 1, 0)]), axis=0)
        split_ref[2 * p] = first_basis
        split_ref[2 * p + 1] = second_basis
        basis = jnp.concatenate([first_basis, second_basis], axis=0)
        high, low = split_parts(xbuf[...])
        total = 0.5 * (dot_nt(high, basis) + dot_nt(low, basis))
        both = []
        for part in (total[:, 0:lanes], total[:, lanes : 2 * lanes]):
            both.append(part + pltpu.roll(part, rank, 1))
        kept = jnp.where(rows < BR * meta_ref[edge + 2 * p + 1], both[0], both[1])
        fac[...] = jnp.where(rows < BR * meta_ref[edge + 2 * p], fac[...], kept)
        return carry

    lax.fori_loop(0, (last - first + 2) // 2, pair_step, 0)
    half = fac.shape[0] // 2
    f_ref[...] = jnp.where(
        upper_half(f_ref.shape), fac[half : 2 * half, :], fac[0:half, :]
    )
    upper = upper_half((BR, lanes)).astype(jnp.int32)
    for k in range(blocks):
        slot = rank_of[k]
        place = pl.ds(pl.multiple_of(lax.shift_right_logical(slot, 1) * BR, BR), BR)
        mine = upper == lax.bitwise_and(slot, 1)
        pltpu.store(send_ref.at[owner_of[k], place, :], fac[BR * k : BR * (k + 1), :], mask=mine)


def project_slabs(ids, owners, diff, bases_t, momentum):
    rows, width = diff.shape
    mats, rank, _ = bases_t.shape
    n_own, peer = momentum.shape[:2]
    pairs, share = send_plan(peer)
    blocks = rows // BR
    hbm = pl.BlockSpec(memory_space=pltpu.HBM)
    vmem = pl.BlockSpec(memory_space=pltpu.VMEM)
    return pl.pallas_call(
        project_kernel,
        out_shape=(
            jax.ShapeDtypeStruct((rows // 2, 2 * rank), jnp.float32),
            jax.ShapeDtypeStruct((n_own, BR * (pairs + share), 2 * rank), jnp.float32),
            jax.ShapeDtypeStruct((mats + mats % 2, 2 * rank, width), jnp.bfloat16),
            jax.ShapeDtypeStruct((meta_size(blocks, mats), 2 * rank), jnp.int32),
        ),
        in_specs=[hbm] * 5,
        out_specs=(vmem,) * 4,
        scratch_shapes=[
            pltpu.SMEM(ids.shape, jnp.int32),
            pltpu.SMEM(owners.shape, jnp.int32),
            pltpu.SMEM((blocks,), jnp.int32),
            pltpu.SMEM((blocks,), jnp.int32),
            pltpu.SMEM((n_own,), jnp.int32),
            pltpu.SMEM((meta_size(blocks, mats),), jnp.int32),
            pltpu.VMEM((rows, width), jnp.float32),
            pltpu.VMEM((2, rank, width), jnp.float32),
            pltpu.VMEM((n_own, 2 * pairs, BR, rank), jnp.float32),
            pltpu.VMEM((rows, 2 * rank), jnp.float32),
            pltpu.SemaphoreType.DMA,
            pltpu.SemaphoreType.DMA,
            pltpu.SemaphoreType.DMA,
            pltpu.SemaphoreType.DMA((2,)),
            pltpu.SemaphoreType.DMA,
        ],
        compiler_params=pltpu.CompilerParams(vmem_limit_bytes=VMEM_LIMIT),
        cost_estimate=pl.CostEstimate(
            flops=6 * rows * width * rank, bytes_accessed=6 << 20, transcendentals=0
        ),
        name="project_slabs",
    )(*[pltpu.with_memory_space_constraint(v, pltpu.HBM) for v in (ids, owners, diff, bases_t, momentum)])


def rebuild_kernel(
    table_ref, fmine_ref, fother_ref, mine_ref, other_ref, mom_ref, w_ref, split_ref,
    nm_hbm, out_hbm, obuf, nbuf, sent, lhs, gath, osem, nsem,
):
    lanes = gath.shape[1]
    rank = lanes // 2
    blocks = gath.shape[0] // BR
    n_own, peer = mom_ref.shape[:2]
    pairs, share = send_plan(peer)
    edge = blocks + 1
    rep = lax.axis_index("rep")

    def o_copy(c):
        cols = pl.ds(COLUMNS[c], COLUMNS[c + 1] - COLUMNS[c])
        return pltpu.make_async_copy(obuf.at[:, cols], out_hbm.at[:, cols], osem.at[c])

    n_copy = pltpu.make_async_copy(nbuf, nm_hbm, nsem)
    span = n_own * BR * share
    for source, ref in ((rep, mine_ref), (1 - rep, other_ref)):
        place = pl.ds(pl.multiple_of(source * span, BR), span)
        sent[place, :] = ref[:, BR * pairs : BR * (pairs + share), :].reshape(span, lanes)
    arrived = mine_ref[:, 0 : BR * pairs, :] + other_ref[:, 0 : BR * pairs, :]
    for s in range(peer):
        block = arrived[:, BR * (s // 2) : BR * (s // 2 + 1), :]
        lane = rank * (s % 2)
        nbuf[:, s] = decay_rate * mom_ref[:, s] + block[:, :, lane : lane + rank]
    n_copy.start()
    average = fmine_ref[...] + fother_ref[...]
    turned = pltpu.roll(average, rank, 1)
    above = upper_half(average.shape)
    placed = jnp.concatenate(
        [jnp.where(above, turned, average), jnp.where(above, average, turned)], axis=0
    )
    upper = upper_half((BR, lanes)).astype(jnp.int32)
    total = table_ref[blocks : blocks + 1, 0:1][0, 0]
    for k in range(blocks):
        odd = lax.bitwise_and(table_ref[k : k + 1, :], 1)
        row = lax.bitwise_and(table_ref[k : k + 1, 0:1][0, 0], -BR)
        tile = sent[pl.ds(pl.multiple_of(row, BR), BR), :]
        gath[BR * k : BR * (k + 1), :] = jnp.where(upper == odd, tile, 0.0)
    picked = gath[...]
    held = decay_rate * (picked + pltpu.roll(picked, rank, 1)) + placed
    step = -outer_rate * (placed + decay_rate * held)
    high = step.astype(jnp.bfloat16).astype(jnp.float32)
    parts = jnp.where(upper_half(step.shape), step - high, high)
    rows = lax.broadcasted_iota(jnp.int32, step.shape, 0)

    def left_rows(t):
        start = BR * table_ref[pl.ds(edge + t, 1), :]
        stop = BR * table_ref[pl.ds(edge + t + 1, 1), :]
        inside = (rows >= start) & (rows < stop)
        return jnp.where(inside, parts, 0.0).astype(jnp.bfloat16)

    left0 = left_rows(0)
    left1 = left_rows(1)
    lhs[0] = left0
    lhs[1] = left1

    @pl.when(total > 2)
    def _():
        def fill(t, carry):
            lhs[t] = left_rows(t)
            return carry

        lax.fori_loop(2, total, fill, 0)

    def right_rows(t, c):
        start, stop = COLUMNS[c], COLUMNS[c + 1]
        top, bottom = split_ref[t, 0:rank, start:stop], split_ref[t, rank : 2 * rank, start:stop]
        return [top, top, bottom, bottom]

    def product(left, right):
        return jnp.dot(
            jnp.concatenate(left, axis=1),
            jnp.concatenate(right, axis=0),
            preferred_element_type=jnp.float32,
        )

    for c in range(len(COLUMNS) - 1):
        cols = slice(COLUMNS[c], COLUMNS[c + 1])

        @pl.when(total == 1)
        def _():
            one = product([lhs[0], lhs[0]], right_rows(0, c))
            obuf[:, cols] = w_ref[:, cols] + one

        @pl.when(total > 1)
        def _():
            two = product(
                [lhs[0], lhs[0], lhs[1], lhs[1]], right_rows(0, c) + right_rows(1, c)
            )
            obuf[:, cols] = w_ref[:, cols] + two

            def add_matrix(t, carry):
                obuf[:, cols] += product([lhs[t], lhs[t]], right_rows(t, c))
                return carry

            lax.fori_loop(2, total, add_matrix, 0)

        o_copy(c).start()
    for c in range(len(COLUMNS) - 1):
        o_copy(c).wait()
    n_copy.wait()


def rebuild_slabs(meta, fmine, fother, mine, other, momentum, weights, split):
    rows, width = weights.shape
    mats, lanes, _ = split.shape
    n_own, peer = momentum.shape[:2]
    _, share = send_plan(peer)
    vmem = pl.BlockSpec(memory_space=pltpu.VMEM)
    hbm = pl.BlockSpec(memory_space=pltpu.HBM)
    return pl.pallas_call(
        rebuild_kernel,
        out_shape=(
            jax.ShapeDtypeStruct(momentum.shape, jnp.float32),
            jax.ShapeDtypeStruct(weights.shape, jnp.float32),
        ),
        in_specs=[vmem] * 8,
        out_specs=(hbm, hbm),
        scratch_shapes=[
            pltpu.VMEM((rows, width), jnp.float32),
            pltpu.VMEM(momentum.shape, jnp.float32),
            pltpu.VMEM((2 * n_own * BR * share, lanes), jnp.float32),
            pltpu.VMEM((mats, rows, lanes), jnp.bfloat16),
            pltpu.VMEM((rows, lanes), jnp.float32),
            pltpu.SemaphoreType.DMA((len(COLUMNS) - 1,)),
            pltpu.SemaphoreType.DMA,
        ],
        compiler_params=pltpu.CompilerParams(vmem_limit_bytes=VMEM_LIMIT),
        cost_estimate=pl.CostEstimate(
            flops=8 * rows * width * lanes, bytes_accessed=8 << 20, transcendentals=0
        ),
        name="rebuild_slabs",
    )(meta, fmine, fother, mine, other, momentum, weights, split)


def per_device(weights, differences, bases, momentum, owners, matrix_ids):
    blocks, br, width = weights.shape
    swap = [(0, 1), (1, 0)]
    bases_t = jnp.swapaxes(bases, 1, 2)
    owner_row = owners.T
    fmine, packed, split, meta = project_slabs(
        matrix_ids, owner_row, differences.reshape(blocks * br, width), bases_t, momentum[0]
    )
    fother = lax.ppermute(fmine, "rep", swap)
    mine = lax.all_to_all(packed, "own", split_axis=0, concat_axis=0, tiled=True)
    other = lax.ppermute(mine, "rep", swap)
    new_momentum, new_weights = rebuild_slabs(
        meta, fmine, fother, mine, other, momentum[0],
        weights.reshape(blocks * br, width), split,
    )
    return (new_weights.reshape(weights.shape), new_momentum[None])


def solution(mesh):
    placed = (
        P("own", None, None),
        P("rep", "own", None, None),
        P(),
        P("own", None, None, None, None),
        P(),
        P(),
    )
    return jax.shard_map(
        per_device,
        mesh=mesh,
        in_specs=placed,
        out_specs=(P("own", None, None), P("own", None, None, None, None)),
        check_vma=False,
    )
```
